128 devices in a mesh: gx: 8 (over x_hi, z), yz: 16 (over x_lo, y, core).
Axes of the slice: x: 4 (x_hi: 2, x_lo: 2; x = x_hi * 2 + x_lo), y: 4, z: 4, core: 2. Of those that a mesh axis runs over, the one named last changes fastest.
Arguments:
- positions: bfloat16 [3, 32768], P(None, ('gx', 'yz')), may hold values from 0 to 1
- species: int32 [32768], P(('gx', 'yz')), may hold values from 0 to 5
- features: bfloat16 [32768, 512], P(('gx', 'yz')), may hold values from -6 to 6
- move_dest: int32 [256], P(('gx', 'yz')), may hold values from 0 to 15, as said below
- move_slot: int32 [256], P(('gx', 'yz')), may hold values from 0 to 1, as said below
- halo_list: int32 [4096], P(('gx', 'yz')), may hold values from 0 to 255
- neighbours: int32 [32768, 64], P(('gx', 'yz')), may hold values from 0 to 383, as said below
- neighbour_count: int32 [32768], P(('gx', 'yz')), may hold values from 16 to 64
- wave_index: int32 [3, 4096], replicated, may hold values from -32 to 32, as said below
- radial_in: bfloat16 [8, 64], replicated, may hold values from -2 to 2
- radial_mid: bfloat16 [2, 64, 64], replicated, may hold values from -0.75 to 0.75
- radial_out: bfloat16 [64, 512], replicated, may hold values from -0.75 to 0.75
- up_weight: bfloat16 [2, 128, 128], replicated, may hold values from -0.5 to 0.5
- prod_weight: float32 [6, 640], replicated, may hold values from -4 to 4
- out_weight: bfloat16 [2, 128, 128], replicated, may hold values from -0.5 to 0.5
- skip_weight: bfloat16 [2, 128, 128], replicated, may hold values from -0.5 to 0.5
- charge_weight: bfloat16 [128, 8], replicated, may hold values from -0.5 to 0.5
- field_weight: float32 [8, 128], replicated, may hold values from -2 to 2
- read_weight: bfloat16 [128, 16], replicated, may hold values from -0.5 to 0.5
- read_vector: float32 [16], replicated, may hold values from -1.5 to 1.5
- force_weight: float32 [128], replicated, may hold values from -0.5 to 0.5
Outputs:
- forces: float32 [3, 32768], P(None, ('gx', 'yz'))
- energies: float32 [32768], P(('gx', 'yz'))
The draws below stay inside these ranges and needn't reach their ends.
Inputs may be any that keep to these rules, and one draw needn't show every extreme that they name: `move_dest`: the destination lies in the same gx row. Exactly 2 blocks of each device go to other devices, at most one to any one device, and each device receives exactly 2 blocks; the others stay. `move_slot`: the 2 blocks that a device holds after the move take its 2 slots once each. `neighbours`: row of the device's table: its working atoms, then the ghosts from gx - 1, gx + 1, yz - 1, yz + 1. Never the atom itself; slots from neighbour_count on are padding. `wave_index`: row 0 runs from 1 to 16, row 1 from -32 to 32, row 2 from -2 to 2.
All inputs are finite; a program needn't handle non-finite values.
Results may differ from the reference program's by a relative error of at most 0.0028.
Values may be sent and summed in bfloat16 or wider, within the bound.
No kernel may reach another device: no remote copies, remote signals or barrier semaphores. Data moves between devices by JAX's collectives and lax.ppermute only.
A program may use at most 64 MiB of HBM per device.

```python
import math
import jax
import jax.numpy as jnp
from jax import lax

C = 128
Q = 8
K = 4096
NRAD = 8
RAD_H = 64
READ_H = 16
NSPEC = 6
MAXNB = 64
BLK = 128
MOVES = 2
A_DEV = 256
HALO = 32
NB_DEV = 2
DOM_X = 8
DOM_Y = 16
ATOMS = 32768
HALOS = 4096


def shuffled_offsets(subkey):
    return jax.random.permutation(subkey, DOM_Y - 1)[:MOVES].astype(jnp.int32) + 1


def shuffled_blocks(subkey):
    return jax.random.permutation(subkey, NB_DEV).astype(jnp.int32)


def plan_tables(key):
    plan_key = jax.random.fold_in(key, 4242)
    key_offsets, key_order, key_slots = jax.random.split(plan_key, 3)
    devices = DOM_X * DOM_Y
    offsets = jax.vmap(shuffled_offsets)(jax.random.split(key_offsets, DOM_X))
    block_order = jax.vmap(shuffled_blocks)(jax.random.split(key_order, devices))
    slot_order = jax.vmap(shuffled_blocks)(jax.random.split(key_slots, devices))
    device_ids = jnp.arange(devices, dtype=jnp.int32)
    row_of = device_ids // DOM_Y
    column_of = device_ids % DOM_Y
    rounds = jnp.arange(NB_DEV, dtype=jnp.int32)
    padded = jnp.concatenate([offsets, jnp.zeros((DOM_X, NB_DEV - MOVES), jnp.int32)], axis=1)
    dest_round = (column_of[:, None] + padded[row_of]) % DOM_Y
    dest_device = row_of[:, None] * DOM_Y + dest_round
    slot_round = slot_order[dest_device, jnp.broadcast_to(rounds[None, :], dest_device.shape)]
    inverse = jnp.argsort(block_order, axis=1).astype(jnp.int32)
    destination = jnp.take_along_axis(dest_round, inverse, axis=1)
    slot_table = jnp.take_along_axis(slot_round, inverse, axis=1)
    return (destination.reshape(-1).astype(jnp.int32), slot_table.reshape(-1).astype(jnp.int32))


def draw_move_dest(key, part):
    return plan_tables(key)[0]


def draw_move_slot(key, part):
    return plan_tables(key)[1]


def draw_neighbours(key, part):
    table_size = A_DEV + 4 * HALO
    drawn_rows = jax.random.randint(jax.random.fold_in(key, 31), (ATOMS, MAXNB), 0, table_size - 1, dtype=jnp.int32)
    own_row = (jnp.arange(ATOMS, dtype=jnp.int32) % A_DEV)[:, None]
    return drawn_rows + (drawn_rows >= own_row).astype(jnp.int32)


def draw_wave_index(key, part):
    subkeys = jax.random.split(jax.random.fold_in(key, 57), 3)
    along_x = jax.random.randint(subkeys[0], (K,), 1, 2 * DOM_X + 1, dtype=jnp.int32)
    along_y = jax.random.randint(subkeys[1], (K,), -2 * DOM_Y, 2 * DOM_Y + 1, dtype=jnp.int32)
    along_z = jax.random.randint(subkeys[2], (K,), -2, 3, dtype=jnp.int32)
    return jnp.stack([along_x, along_y, along_z])


def place_ends(result, key, low, top_value):
    longest = result.shape.index(max(result.shape))
    spots = []
    for shift in (0, 1):
        where = [jax.random.randint(jax.random.fold_in(key, axis), (), 0, length) for axis, length in enumerate(result.shape)]
        where[longest] = (where[longest] + shift) % result.shape[longest]
        spots.append(tuple(where))
    return result.at[spots[0]].set(low).at[spots[1]].set(top_value)


def steps_of(rng, dims, cuts, low, largest):
    level, own = 1.0, jax.random.fold_in(rng, 6)
    for dim, shards_of in cuts:
        steps = jnp.exp(jax.random.uniform(jax.random.fold_in(own, dim), (shards_of,), jnp.float32, low / len(cuts), largest / len(cuts)))
        level = level * jnp.repeat(steps, dims[dim] // shards_of).reshape([-1 if axis == dim else 1 for axis in range(len(dims))])
    return level


def gaussian(key, extent, spread, bound, cuts=(), held_as=jnp.bfloat16):
    gain = steps_of(key, extent, cuts, -0.22, 0.18) if cuts else 1.0
    values = jax.random.normal(key, extent, jnp.float32) * spread * gain
    return jnp.minimum(jnp.maximum(values, -bound), bound).astype(held_as)


def setup_inputs(seed: int = 0) -> dict:
    keys = jax.random.split(jax.random.key(seed), 22)
    positions = jnp.clip(1.0 * jax.random.uniform(keys[0], (3, ATOMS), jnp.float32) ** steps_of(keys[0], (3, ATOMS), ((1, 128),), -0.2, 0.2), 0.0, 1.0).astype(jnp.bfloat16)
    species = place_ends(jax.random.randint(keys[1], (ATOMS,), 0, NSPEC), jax.random.fold_in(keys[1], 1), 0, NSPEC - 1).astype(jnp.int32)
    features = gaussian(keys[2], (ATOMS, 4 * C), 1.0, 6.0, ((0, 128),))
    move_dest = draw_move_dest(jax.random.fold_in(keys[21], 71), 0)
    move_slot = draw_move_slot(jax.random.fold_in(keys[21], 71), 0)
    halo_list = place_ends(jax.random.randint(keys[5], (HALOS,), 0, A_DEV), jax.random.fold_in(keys[5], 1), 0, A_DEV - 1).astype(jnp.int32)
    neighbours = draw_neighbours(jax.random.fold_in(keys[21], 71), 0)
    neighbour_count = place_ends(jax.random.randint(keys[7], (ATOMS,), MAXNB // 4, MAXNB + 1), jax.random.fold_in(keys[7], 1), MAXNB // 4, MAXNB).astype(jnp.int32)
    wave_index = draw_wave_index(jax.random.fold_in(keys[21], 71), 0)
    radial_in = gaussian(keys[9], (NRAD, RAD_H), NRAD ** -0.5, 2.0)
    radial_mid = gaussian(keys[10], (2, RAD_H, RAD_H), RAD_H ** -0.5, 0.75)
    radial_out = gaussian(keys[11], (RAD_H, 4 * C), RAD_H ** -0.5, 0.75)
    up_weight = gaussian(keys[12], (2, C, C), C ** -0.5, 0.5)
    prod_weight = gaussian(keys[13], (NSPEC, 5 * C), 0.7, 4.0, (), jnp.float32)
    out_weight = gaussian(keys[14], (2, C, C), C ** -0.5, 0.5)
    skip_weight = gaussian(keys[15], (2, C, C), C ** -0.5, 0.5)
    charge_weight = gaussian(keys[16], (C, Q), C ** -0.5, 0.5)
    field_weight = gaussian(keys[17], (Q, C), Q ** -0.5, 2.0, (), jnp.float32)
    read_weight = gaussian(keys[18], (C, READ_H), C ** -0.5, 0.5)
    read_vector = gaussian(keys[19], (READ_H,), READ_H ** -0.5, 1.5, (), jnp.float32)
    force_weight = gaussian(keys[20], (C,), C ** -0.5, 0.5, (), jnp.float32)
    return dict(positions=positions, species=species, features=features, move_dest=move_dest, move_slot=move_slot, halo_list=halo_list, neighbours=neighbours, neighbour_count=neighbour_count, wave_index=wave_index, radial_in=radial_in, radial_mid=radial_mid, radial_out=radial_out, up_weight=up_weight, prod_weight=prod_weight, out_weight=out_weight, skip_weight=skip_weight, charge_weight=charge_weight, field_weight=field_weight, read_weight=read_weight, read_vector=read_vector, force_weight=force_weight)


highest = lax.Precision.HIGHEST
two_pi = 2.0 * math.pi
cutoff_radius = 3.5
basis_sharpness = 4.0
ewald_width = 0.1
ewald_scale = 0.01
atom_step = 64
wave_step = 512

def wave_vectors(wave_index, domains_x, domains_y):
    scales = jnp.array([two_pi / domains_x, two_pi / domains_y, two_pi], jnp.float32)
    wavevectors = wave_index.astype(jnp.float32) * scales[:, None]
    squared = lax.optimization_barrier(jnp.sum(wavevectors * wavevectors, axis=0))
    prefactor = 8.0 * math.pi * ewald_scale / (domains_x * domains_y)
    weights = prefactor * jnp.exp(-0.5 * ewald_width * ewald_width * squared) / squared
    return (wavevectors, weights)

def phase_of(absolute, wavevectors):
    return absolute[0][:, None] * wavevectors[0][None, :] + absolute[1][:, None] * wavevectors[1][None, :] + absolute[2][:, None] * wavevectors[2][None, :]

def structure_terms(absolute, charges, wavevectors):
    stride = math.gcd(wavevectors.shape[1], wave_step)
    block_count = wavevectors.shape[1] // stride

    def one_block(block_index):
        wave_block = lax.dynamic_slice_in_dim(wavevectors, block_index * stride, stride, 1)
        phases = phase_of(absolute, wave_block)
        real_part = jnp.einsum('ak,aq->kq', jnp.cos(phases), charges, precision=highest)
        imag_part = jnp.einsum('ak,aq->kq', jnp.sin(phases), charges, precision=highest)
        return (real_part, imag_part)
    real_part, imag_part = lax.map(one_block, jnp.arange(block_count, dtype=jnp.int32))
    latent = charges.shape[1]
    return (real_part.reshape(-1, latent), imag_part.reshape(-1, latent))

def field_terms(absolute, wavevectors, weights, total_real, total_imag):
    scaled_real = weights[:, None] * total_real
    scaled_imag = weights[:, None] * total_imag
    right_cos = jnp.concatenate([scaled_real] + [-wavevectors[direction][:, None] * scaled_imag for direction in range(3)], axis=1)
    right_sin = jnp.concatenate([scaled_imag] + [wavevectors[direction][:, None] * scaled_real for direction in range(3)], axis=1)
    stride = math.gcd(wavevectors.shape[1], wave_step)
    block_count = wavevectors.shape[1] // stride

    def accumulate(block_index, running):
        wave_block = lax.dynamic_slice_in_dim(wavevectors, block_index * stride, stride, 1)
        phases = phase_of(absolute, wave_block)
        cos_right = lax.dynamic_slice_in_dim(right_cos, block_index * stride, stride, 0)
        sin_right = lax.dynamic_slice_in_dim(right_sin, block_index * stride, stride, 0)
        running = running + jnp.dot(jnp.cos(phases), cos_right, precision=highest)
        return running + jnp.dot(jnp.sin(phases), sin_right, precision=highest)
    initial = jnp.zeros((absolute.shape[1], right_cos.shape[1]), jnp.float32)
    return lax.fori_loop(0, block_count, accumulate, initial)

def project_pair(feature, weights):
    channels = weights.shape[1]
    row_count = feature.shape[0]
    scalar = jnp.dot(feature[:, :channels], weights[0], preferred_element_type=jnp.float32)
    vector = jnp.dot(feature[:, channels:].reshape(row_count * 3, channels), weights[1], preferred_element_type=jnp.float32)
    return jnp.concatenate([scalar, vector.reshape(row_count, 3 * channels)], axis=1)

def edge_products(table_pos, table_up, centre_pos, nbr_rows, nbr_live, coeffs, radial_in, radial_mid, radial_out):
    atom_count, slot_count = nbr_rows.shape
    edge_count = atom_count * slot_count
    flat_rows = nbr_rows.reshape(edge_count)
    offset = (table_pos[:, flat_rows].reshape(3, atom_count, slot_count) - centre_pos[:, :, None]).reshape(3, edge_count)
    distance = jnp.sqrt(lax.optimization_barrier(jnp.sum(offset * offset, axis=0)))
    scaled_dist = distance / cutoff_radius
    envelope = 1.0 - 28.0 * scaled_dist ** 6 + 48.0 * scaled_dist ** 7 - 21.0 * scaled_dist ** 8
    alive_mask = (jnp.arange(slot_count, dtype=jnp.int32)[None, :] < nbr_live[:, None]).astype(jnp.float32).reshape(edge_count)
    basis_count = radial_in.shape[0]
    centres = jnp.arange(basis_count, dtype=jnp.float32) * (cutoff_radius / (basis_count - 1))
    radial_basis = jnp.exp(-basis_sharpness * (distance[:, None] - centres[None, :]) ** 2).astype(jnp.bfloat16)
    hidden = jax.nn.silu(jnp.dot(radial_basis, radial_in, preferred_element_type=jnp.float32)).astype(jnp.bfloat16)
    hidden = jax.nn.silu(jnp.dot(hidden, radial_mid[0], preferred_element_type=jnp.float32)).astype(jnp.bfloat16)
    hidden = jax.nn.silu(jnp.dot(hidden, radial_mid[1], preferred_element_type=jnp.float32)).astype(jnp.bfloat16)
    radial = (jnp.dot(hidden, radial_out, preferred_element_type=jnp.float32) * (envelope * alive_mask)[:, None]).astype(jnp.bfloat16)
    channels = radial.shape[1] // 4
    gathered = table_up[flat_rows]

    def column_block(source, number):
        return source[:, number * channels:(number + 1) * channels].astype(jnp.float32)
    norm_factor = 1.0 / math.sqrt(slot_count)

    def neighbour_sum(values):
        return lax.optimization_barrier(jnp.sum(values.reshape(atom_count, slot_count, channels), axis=1)) * norm_factor
    up_scalar = column_block(gathered, 0)
    up_vector = [column_block(gathered, 1 + direction) for direction in range(3)]
    along = up_vector[0] * offset[0][:, None] + up_vector[1] * offset[1][:, None] + up_vector[2] * offset[2][:, None]
    scalar_msg = neighbour_sum(column_block(radial, 0) * up_scalar + column_block(radial, 1) * along)
    radial_scalar = column_block(radial, 2) * up_scalar
    radial_vector = column_block(radial, 3)
    vector_msg = [neighbour_sum(radial_scalar * offset[direction][:, None] + radial_vector * up_vector[direction]) for direction in range(3)]
    square_sum = vector_msg[0] * vector_msg[0] + vector_msg[1] * vector_msg[1] + vector_msg[2] * vector_msg[2]
    path_weights = [coeffs[:, number * channels:(number + 1) * channels] for number in range(5)]
    scalar_prod = path_weights[0] * scalar_msg + path_weights[1] * scalar_msg * scalar_msg + path_weights[2] * square_sum
    vector_prod = [path_weights[3] * vector_msg[direction] + path_weights[4] * scalar_msg * vector_msg[direction] for direction in range(3)]
    return jnp.concatenate([scalar_prod] + vector_prod, axis=1).astype(jnp.bfloat16)

def atom_results(work_feat, products, charges, efield, out_weight, skip_weight, field_weight, read_weight, read_vector, force_weight):
    channels = out_weight.shape[1]
    latent = charges.shape[1]
    mixed_feat = project_pair(products, out_weight) + project_pair(work_feat, skip_weight)
    potential = efield[:, :latent]
    scalars = mixed_feat[:, :channels] + jnp.dot(potential, field_weight, precision=highest)
    readout = jax.nn.silu(jnp.dot(scalars.astype(jnp.bfloat16), read_weight, preferred_element_type=jnp.float32))
    energy = jnp.dot(readout, read_vector, precision=highest) + 0.5 * lax.optimization_barrier(jnp.sum(charges * potential, axis=1))
    forces = [jnp.dot(mixed_feat[:, (1 + direction) * channels:(2 + direction) * channels], force_weight, precision=highest) + lax.optimization_barrier(jnp.sum(charges * efield[:, (1 + direction) * latent:(2 + direction) * latent], axis=1)) for direction in range(3)]
    return jnp.stack(forces + [energy])

def take_columns(matrix, chosen):
    return matrix[:, chosen]

def take_rows(matrix, chosen):
    return matrix[chosen]

def reference(positions, species, features, move_dest, move_slot, halo_list, neighbours, neighbour_count, wave_index, radial_in, radial_mid, radial_out, up_weight, prod_weight, out_weight, skip_weight, charge_weight, field_weight, read_weight, read_vector, force_weight):
    devices = DOM_X * DOM_Y
    blocks = NB_DEV
    channels = C
    home_device = jnp.arange(devices * blocks, dtype=jnp.int32) // blocks
    target = ((home_device // DOM_Y * DOM_Y + move_dest) * blocks + move_slot).astype(jnp.int32)
    pos_blocks = positions.astype(jnp.float32).reshape(3, devices * blocks, BLK)
    work_pos = jnp.zeros_like(pos_blocks).at[:, target].set(pos_blocks).reshape(3, devices, A_DEV).transpose(1, 0, 2)
    spec_blocks = species.reshape(devices * blocks, BLK)
    work_species = jnp.zeros_like(spec_blocks).at[target].set(spec_blocks).reshape(devices, A_DEV)
    feat_blocks = features.reshape(devices * blocks, BLK, 4 * channels)
    work_feat = jnp.zeros_like(feat_blocks).at[target].set(feat_blocks).reshape(devices, A_DEV, 4 * channels)
    send_lists = halo_list.reshape(devices, HALO)
    send_pos = jax.vmap(take_columns)(work_pos, send_lists).reshape(DOM_X, DOM_Y, 3, HALO)
    send_feat = jax.vmap(take_rows)(work_feat, send_lists).reshape(DOM_X, DOM_Y, HALO, 4 * channels)
    unit_axes = jnp.eye(3, dtype=jnp.float32)
    ghost_pos = [jnp.roll(send_pos, 1, axis=0) - unit_axes[0][:, None], jnp.roll(send_pos, -1, axis=0) + unit_axes[0][:, None], jnp.roll(send_pos, 1, axis=1) - unit_axes[1][:, None], jnp.roll(send_pos, -1, axis=1) + unit_axes[1][:, None]]
    ghost_feat = [jnp.roll(send_feat, 1, axis=0), jnp.roll(send_feat, -1, axis=0), jnp.roll(send_feat, 1, axis=1), jnp.roll(send_feat, -1, axis=1)]
    table_pos = jnp.concatenate([work_pos] + [ghost.reshape(devices, 3, HALO) for ghost in ghost_pos], axis=2)
    table_feat = jnp.concatenate([work_feat] + [ghost.reshape(devices, HALO, 4 * channels) for ghost in ghost_feat], axis=1)
    device_ids = jnp.arange(devices, dtype=jnp.int32)
    anchor = jnp.stack([(device_ids // DOM_Y).astype(jnp.float32), (device_ids % DOM_Y).astype(jnp.float32), jnp.zeros((devices,), jnp.float32)], axis=1)
    absolute = work_pos + anchor[:, :, None]
    charges = jnp.dot(work_feat[:, :, :channels].reshape(devices * A_DEV, channels), charge_weight, preferred_element_type=jnp.float32).reshape(devices, A_DEV, Q)
    wavevectors, weights = wave_vectors(wave_index, DOM_X, DOM_Y)

    def add_device(running, inputs):
        part_real, part_imag = structure_terms(inputs[0], inputs[1], wavevectors)
        return ((running[0] + part_real, running[1] + part_imag), None)
    initial = (jnp.zeros((K, Q), jnp.float32), jnp.zeros((K, Q), jnp.float32))
    (total_real, total_imag), ignored = lax.scan(add_device, initial, (absolute, charges))

    def one_device(inputs):
        tab_pos, tab_feat, own_pos, own_abs, own_species, own_feat, nbr_rows, nbr_live, own_charges = inputs
        table_up = project_pair(tab_feat, up_weight).astype(jnp.bfloat16)
        onehot = (own_species[:, None] == jnp.arange(NSPEC, dtype=jnp.int32)[None, :]).astype(jnp.float32)
        coeffs = jnp.dot(onehot, prod_weight, precision=highest)
        block_count = A_DEV // atom_step

        def edge_block(pieces):
            return edge_products(tab_pos, table_up, pieces[2], pieces[0], pieces[1], pieces[3], radial_in, radial_mid, radial_out)
        products = lax.map(edge_block, (nbr_rows.reshape(block_count, atom_step, MAXNB), nbr_live.reshape(block_count, atom_step), own_pos.reshape(3, block_count, atom_step).transpose(1, 0, 2), coeffs.reshape(block_count, atom_step, 5 * channels))).reshape(A_DEV, 4 * channels)
        efield = field_terms(own_abs, wavevectors, weights, total_real, total_imag)
        return atom_results(own_feat, products, own_charges, efield, out_weight, skip_weight, field_weight, read_weight, read_vector, force_weight)
    results = lax.map(one_device, (table_pos, table_feat, work_pos, absolute, work_species, work_feat, neighbours.reshape(devices, A_DEV, MAXNB), neighbour_count.reshape(devices, A_DEV), charges))
    res_blocks = results.reshape(devices, 4, blocks, BLK).transpose(1, 0, 2, 3).reshape(4, devices * blocks, BLK)
    home_res = res_blocks[:, target].reshape(4, devices * A_DEV)
    return (home_res[:3], home_res[3])
```

```python
import math

import jax
import jax.numpy as jnp
from jax import lax
from jax.experimental import pallas as pl
from jax.experimental.pallas import tpu as pltpu
from jax.sharding import PartitionSpec as P

f32, bf16, i32 = jnp.float32, jnp.bfloat16, jnp.int32
highest = lax.Precision.HIGHEST
two_pi = 2.0 * math.pi
cutoff_radius = 3.5
ewald_width = 0.1
ewald_scale = 0.01

NX, NY, NZ = 16, 32, 2
SLABS = 2 * NZ + 2
SLOT_GROUP = 4


def dot(a, b, ca, cb, precision=None):
    return lax.dot_general(
        a, b, (((ca,), (cb,)), ((), ())), precision=precision, preferred_element_type=f32
    )


def silu(v):
    half = 0.5 * v
    return half + half * jnp.tanh(half)


def iota(shape, dim):
    return lax.broadcasted_iota(i32, shape, dim)


def turns(t):
    angle = two_pi * (t - jnp.floor(t + 0.5))
    return jnp.cos(angle), jnp.sin(angle)


def params(vmem=32):
    return pltpu.CompilerParams(vmem_limit_bytes=vmem << 20)


def cost(flops, transcendentals, moved):
    return pl.CostEstimate(flops=flops, transcendentals=transcendentals, bytes_accessed=moved)


SMEM = pl.BlockSpec(memory_space=pltpu.SMEM)


def up_kernel(feat, up, charge_weight, out, charges):
    charges[...] = dot(charge_weight[...], feat[:, 0:128], 1, 1)
    for b in range(2):
        for c in range(4):
            rows = feat[b * 128 : (b + 1) * 128, c * 128 : (c + 1) * 128]
            mapped = dot(up[min(c, 1)], rows, 0, 1).astype(bf16)
            out[b, c * 128 : (c + 1) * 128, :] = mapped


def moment_kernel(
    dest, slot, place, charges_in, pos, species, halo, out, basis, waves, stage
):
    gx = place[0].astype(f32)
    charges = charges_in[...]
    lane = iota((1, 256), 1)
    second = lane >= 128
    xyz = pos[...].astype(f32)
    along_x = xyz[0:1] + gx
    along_y = xyz[1:2] + jnp.where(second, dest[1], dest[0]).astype(f32)
    along_z = xyz[2:3]
    cos_x, sin_x = turns((iota((NX, 256), 0) + 1).astype(f32) * along_x * (1.0 / 8.0))
    cos_y, sin_y = turns((iota((NY, 256), 0) + 1).astype(f32) * along_y * (1.0 / 16.0))
    cos_z, sin_z = turns(iota((8, 256), 0).astype(f32) * along_z)
    pairs = [
        (cos_z[abs(z) : abs(z) + 1], sin_z[abs(z) : abs(z) + 1] * (1.0 if z >= 0 else -1.0))
        for z in range(-NZ, NZ + 1)
    ]
    for i, (c, s) in enumerate(pairs):
        at = i * 128
        basis[at : at + 32, 0:256] = cos_y * c
        basis[at + 32 : at + 64, 0:256] = sin_y * c
        basis[at + 64 : at + 96, 0:256] = cos_y * s
        basis[at + 96 : at + 128, 0:256] = sin_y * s
        basis[at : at + 32, 256:512] = -(cos_y * s)
        basis[at + 32 : at + 64, 256:512] = -(sin_y * s)
        basis[at + 64 : at + 96, 256:512] = cos_y * c
        basis[at + 96 : at + 128, 256:512] = sin_y * c
    at = 128 * (SLABS - 1)
    basis[at : at + 128, :] = jnp.zeros((128, 512), f32)
    for i, (c, s) in enumerate(pairs):
        basis[at + i : at + i + 1, 0:256] = c
        basis[at + i : at + i + 1, 256:512] = -s
        basis[at + 64 + i : at + 65 + i, 0:256] = s
        basis[at + 64 + i : at + 65 + i, 256:512] = c
    waves[0:8] = charges
    waves[8:24] = cos_x
    waves[24:40] = sin_x
    left_cos = (cos_x[:, None, :] * charges[None]).reshape(128, 256)
    left_sin = (sin_x[:, None, :] * charges[None]).reshape(128, 256)
    moments = dot(left_cos, basis[:, 0:256], 1, 1, highest) + dot(
        left_sin, basis[:, 256:512], 1, 1, highest
    )
    for i in range(SLABS):
        stage[:, i, :] = moments[:, i * 128 : (i + 1) * 128]
    kinds = species[...].astype(f32)
    for b in range(2):
        cut = slice(b * 128, (b + 1) * 128)
        for m in range(3):
            stage[:, 6 + 3 * b + m, :] = jnp.broadcast_to(xyz[m : m + 1, cut], (128, 128))
        stage[:, 12 + b, :] = jnp.broadcast_to(kinds[:, cut], (128, 128))
    listed = jnp.concatenate([halo[...], jnp.zeros((1, 96), i32)], axis=1)
    at = iota((1, 128), 1)
    for b in range(2):
        listed = jnp.where(at == 32 + b, dest[b], listed)
        listed = jnp.where(at == 34 + b, slot[b], listed)
    stage[:, 14, :] = jnp.broadcast_to(listed.astype(f32), (128, 128))
    stage[:, 15, :] = jnp.zeros((128, 128), f32)
    out[...] = stage[...].astype(bf16)


def weight_kernel(place, sent, wave_index, out):
    total = jnp.sum(sent[...].astype(f32), axis=0)[0:8]
    own_x = (place[0] * 16 + place[1]) // 8 + 1
    kx, ky, kz = wave_index[0:1, :], wave_index[1:2, :], wave_index[2:3, :]
    count = kx.shape[1]
    ours = kx == own_x
    rank = iota((8, count), 0)
    z_rows = jnp.where(ours & (kz == rank - NZ), 1.0, 0.0).astype(bf16)
    flat_rows = jnp.where(ours & (ky == 0) & (rank == SLABS - 1), 1.0, 0.0).astype(bf16)
    z_any = jnp.where(kz == rank - NZ, 1.0, 0.0).astype(bf16)
    y_match = jnp.where(jnp.abs(ky) == iota((NY, count), 0) + 1, 1.0, 0.0)
    y_sign = jnp.where(ky < 0, -y_match, y_match)
    even = dot(z_rows, y_match.astype(bf16), 1, 1)
    odd = dot(z_rows, y_sign.astype(bf16), 1, 1)
    flat = dot(flat_rows, z_any, 1, 1)
    gap = jnp.zeros((8, 56), f32)
    even = jnp.concatenate([even] * 4, axis=1)
    odd = jnp.concatenate([odd] * 4, axis=1)
    flat = jnp.concatenate([flat, gap] * 2, axis=1)
    row, lane = iota((8, 128), 0), iota((8, 128), 1)
    in_flat = row == SLABS - 1
    x_wave = own_x.astype(f32) * (two_pi / 8.0)
    y_wave = jnp.where(in_flat, 0, lane % 32 + 1).astype(f32) * (two_pi / 16.0)
    z_wave = (jnp.where(in_flat, lane % 64, row) - NZ).astype(f32) * two_pi
    squared = x_wave * x_wave + y_wave * y_wave + z_wave * z_wave
    prefactor = 8.0 * math.pi * ewald_scale / 128.0
    weight = prefactor * jnp.exp(-0.5 * ewald_width * ewald_width * squared) / squared
    direct = weight * jnp.where(in_flat, flat, even)
    crossed = weight * jnp.where(in_flat, 0.0, odd)
    total = jnp.where(row < SLABS, total, 0.0)
    far = pltpu.roll(total, 64, 1)
    group = lane // 32
    swapped = jnp.where(group % 2 == 0, pltpu.roll(far, 96, 1), pltpu.roll(far, 32, 1))
    swapped = jnp.where((group == 0) | (group == 3), -swapped, swapped)
    coefficient = total * direct + swapped * crossed
    out[...] = jnp.broadcast_to(coefficient[None], out.shape)


def field_kernel(
    coeffs,
    basis,
    waves,
    feat,
    skip_weight,
    field_weight,
    read_weight,
    force_weight,
    out,
    stacked,
):
    lane = iota((128, 128), 1)
    group_even = (lane // 32) % 2 == 0
    low_half = lane < 64
    y_wave = (lane % 32 + 1).astype(f32) * (two_pi / 16.0)
    for i in range(SLABS):
        cut = slice(i * 128, (i + 1) * 128)
        c = coeffs[:, i, :]
        stacked[0:128, cut] = c
        half = pltpu.roll(c, 64, 1)
        if i < SLABS - 1:
            moved = jnp.where(group_even, pltpu.roll(c, 96, 1), -pltpu.roll(c, 32, 1))
            stacked[128:256, cut] = y_wave * moved
            z_wave = two_pi * (i - NZ)
        else:
            stacked[128:256, cut] = jnp.zeros((128, 128), f32)
            z_wave = (lane % 64 - NZ).astype(f32) * two_pi
        stacked[256:384, cut] = z_wave * jnp.where(low_half, half, -half)
    grid = dot(stacked[...], basis[...], 1, 0, highest)
    charges = waves[0:8]
    cos_x = jnp.broadcast_to(waves[8:24][:, None, :], (NX, 8, 256)).reshape(128, 256)
    sin_x = jnp.broadcast_to(waves[24:40][:, None, :], (NX, 8, 256)).reshape(128, 256)
    x_wave = (iota((128, 256), 0) // 8 + 1).astype(f32) * (two_pi / 8.0)

    def channels(v):
        return jnp.sum(v.reshape(NX, 8, 256), axis=0)

    def even_part(at):
        return channels(cos_x * grid[at : at + 128, 0:256] + sin_x * grid[at : at + 128, 256:512])

    potential = even_part(0)
    field = [
        channels(x_wave * (sin_x * grid[0:128, 0:256] - cos_x * grid[0:128, 256:512])),
        -even_part(128),
        -even_part(256),
    ]
    scalars = dot(field_weight[...], potential, 0, 0, highest) + dot(
        skip_weight[0], feat[:, 0:128], 0, 1
    )
    out[0:16] = dot(read_weight[...].astype(f32), scalars, 1, 0, highest)
    for m in range(3):
        vector = dot(skip_weight[1], feat[:, (m + 1) * 128 : (m + 2) * 128], 0, 1)
        out[16 + m : 17 + m] = dot(force_weight[...], vector, 1, 0, highest) + jnp.sum(
            charges * field[m], axis=0, keepdims=True
        )
    out[19:20] = 0.5 * jnp.sum(charges * potential, axis=0, keepdims=True)
    out[20:24] = jnp.zeros((4, 256), f32)


def radial_kernel(
    place,
    sent,
    neighbours,
    live,
    radial_in,
    radial_mid,
    hidden_out,
    offset_out,
    kinds_out,
    home_out,
    stage,
    dist_stage,
    scale_stage,
):
    stage[...] = sent[...].astype(f32)
    gx, yz = place[0], place[1]
    targets = [
        (gx, yz),
        ((gx + 7) % 8, yz),
        ((gx + 1) % 8, yz),
        (gx, (yz + 15) % 16),
        (gx, (yz + 1) % 16),
    ]
    plan = jnp.transpose(stage[:, 14, :])
    row = iota((16, 128), 0)
    device = iota((16, 128), 1)
    want_x, want_y = jnp.full((16, 128), -1, i32), jnp.full((16, 128), -1, i32)
    for t, (tx, ty) in enumerate(targets):
        want_x = jnp.where(row // 2 == t, tx, want_x)
        want_y = jnp.where(row // 2 == t, ty, want_y)
    here = (device // 16 == want_x).astype(f32)
    want_y, want_slot = want_y.astype(f32), (row % 2).astype(f32)
    picks = []
    for b in range(2):
        match = (plan[32 + b : 33 + b] == want_y) & (plan[34 + b : 35 + b] == want_slot)
        picks.append(jnp.where(match, here, 0.0))

    def from_home(first, step):
        return dot(picks[0], stage[:, first, :], 1, 0, highest) + dot(
            picks[1], stage[:, first + step, :], 1, 0, highest
        )

    xyz = [from_home(6 + m, 3) for m in range(3)]
    kinds = from_home(12, 1)
    kinds_out[...] = jnp.concatenate([kinds[0:1], kinds[1:2]], axis=1)
    both = picks[0] + picks[1]
    for s in range(2):
        column = 2.0 * both * (device % 16).astype(f32) + picks[1]
        home_out[s] = jnp.sum(jnp.where(row == s, column, 0.0)).astype(i32)
    lane = iota((1, 128), 1)
    atom = iota((128, 128), 0)
    ghosts = jnp.zeros((8, 128), f32)
    for t, (tx, ty) in enumerate(targets[1:]):
        listed = stage[tx * 16 + ty, 14:15, :].astype(i32)
        if t:
            listed = pltpu.roll(listed, 32 * t, 1)
        listed = jnp.where(lane // 32 == t, listed, -1)
        for s in range(2):
            at = 2 * (t + 1) + s
            rows = jnp.concatenate(
                [x[at : at + 1] for x in xyz] + [jnp.zeros((5, 128), f32)], axis=0
            )
            chosen = jnp.where(atom + 128 * s == listed, 1.0, 0.0)
            ghosts = ghosts + dot(rows, chosen, 1, 0, highest)
    part = lane // 32
    shifts = [
        jnp.where(part == 0, -1.0, jnp.where(part == 1, 1.0, 0.0)),
        jnp.where(part == 2, -1.0, jnp.where(part == 3, 1.0, 0.0)),
        jnp.zeros((1, 128), f32),
    ]
    tables = [
        [
            jnp.broadcast_to(v, (8, 128))
            for v in (xyz[m][0:1], xyz[m][1:2], ghosts[m : m + 1] + shifts[m])
        ]
        for m in range(3)
    ]
    for n in range(0, 64, 8):
        for half in range(2):
            cut = slice(half * 128, (half + 1) * 128)
            index = neighbours[n : n + 8, cut]
            within, block = index & 127, index >> 7
            squared = jnp.zeros((8, 128), f32)
            for m in range(3):
                found = [
                    jnp.take_along_axis(table, within, axis=1, mode="promise_in_bounds")
                    for table in tables[m]
                ]
                picked = jnp.where(block == 0, found[0], jnp.where(block == 1, found[1], found[2]))
                offset = picked - tables[m][half]
                offset_out[m, n : n + 8, cut] = offset
                squared = squared + offset * offset
            dist = jnp.sqrt(squared)
            dist_stage[n : n + 8, cut] = dist
            u = dist * (1.0 / cutoff_radius)
            u6 = (u * u) * (u * u) * (u * u)
            envelope = 1.0 + u6 * (-28.0 + u * (48.0 - 21.0 * u))
            alive = iota((8, 128), 0) + n < live[:, cut]
            scale_stage[n : n + 8, cut] = jnp.where(alive, 0.125 * envelope, 0.0)
    first = jnp.transpose(radial_in[...].astype(f32)).astype(bf16)
    mid = [jnp.transpose(radial_mid[i].astype(f32)).astype(bf16) for i in range(2)]
    centre = iota((8, 256), 0).astype(f32) * (cutoff_radius / 7.0)

    def body(group, carry):
        start = group * SLOT_GROUP
        rows = []
        for j in range(SLOT_GROUP):
            away = dist_stage[pl.ds(start + j, 1), :] - centre
            rows.append(jnp.exp(-4.0 * (away * away)))
        hidden = silu(dot(first, jnp.concatenate(rows, axis=1).astype(bf16), 1, 0)).astype(bf16)
        hidden = silu(dot(mid[0], hidden, 1, 0)).astype(bf16)
        hidden = silu(dot(mid[1], hidden, 1, 0))
        for j in range(SLOT_GROUP):
            scaled = hidden[:, j * 256 : (j + 1) * 256] * scale_stage[pl.ds(start + j, 1), :]
            hidden_out[start + j] = scaled.astype(bf16)
        return carry

    lax.fori_loop(0, 64 // SLOT_GROUP, body, 0)


def halo_kernel(home, first, second, halo, out):
    atom = iota((128, 32), 0)
    chosen = [jnp.where(atom + 128 * s == halo[...], 1.0, 0.0).astype(bf16) for s in range(2)]
    out[...] = (dot(chosen[0], first[0], 0, 1) + dot(chosen[1], second[0], 0, 1)).astype(bf16)


def message_kernel(
    home,
    first,
    second,
    ghost0,
    ghost1,
    ghost2,
    ghost3,
    neighbours,
    offsets,
    hidden,
    kinds,
    radial_out,
    prod_weight,
    out_weight,
    read_weight,
    force_weight,
    out,
    table,
    total,
):
    table[:, 0:128] = first[0]
    table[:, 128:256] = second[0]
    for t, ghost in enumerate((ghost0, ghost1, ghost2, ghost3)):
        table[:, 256 + 32 * t : 288 + 32 * t] = jnp.transpose(ghost[...].astype(f32)).astype(bf16)
    spread = jnp.transpose(radial_out[...].astype(f32)).astype(bf16)
    total[...] = jnp.zeros((512, 256), f32)
    place = iota((384, 256), 0)

    def body(n, carry):
        chosen = jnp.where(place == neighbours[pl.ds(n, 1), :], 1.0, 0.0).astype(bf16)
        radial = dot(spread, hidden[n], 1, 0)
        up = dot(table[...], chosen, 1, 0)
        u0, u1 = up[0:128], [up[128 * m : 128 * (m + 1)] for m in (1, 2, 3)]
        r = [offsets[m, pl.ds(n, 1), :] for m in range(3)]
        along = u1[0] * r[0] + u1[1] * r[1] + u1[2] * r[2]
        total[0:128] += radial[0:128] * u0 + radial[128:256] * along
        scalar = radial[256:384] * u0
        for m in range(3):
            total[128 * (m + 1) : 128 * (m + 2)] += scalar * r[m] + radial[384:512] * u1[m]
        return carry

    lax.fori_loop(0, 64, body, 0, unroll=2)
    kind = jnp.where(iota((6, 256), 0).astype(f32) == kinds[...], 1.0, 0.0)
    paths = dot(prod_weight[...], kind, 0, 0, highest)
    p = [paths[128 * i : 128 * (i + 1)] for i in range(5)]
    a0, a1 = total[0:128], [total[128 * m : 128 * (m + 1)] for m in (1, 2, 3)]
    square = a1[0] * a1[0] + a1[1] * a1[1] + a1[2] * a1[2]
    b0 = (p[0] * a0 + p[1] * a0 * a0 + p[2] * square).astype(bf16)
    rows = [dot(read_weight[...].astype(f32), dot(out_weight[0], b0, 0, 0), 1, 0, highest)]
    for m in range(3):
        b1 = (p[3] * a1[m] + p[4] * a0 * a1[m]).astype(bf16)
        rows.append(dot(force_weight[...], dot(out_weight[1], b1, 0, 0), 1, 0, highest))
    rows.append(jnp.zeros((5, 256), f32))
    result = jnp.concatenate(rows, axis=0)
    out[...] = jnp.zeros(out.shape, f32)
    for s in range(2):
        out[home[s] // 2] = result[:, s * 128 : (s + 1) * 128]


def final_kernel(dest, sent, own, read_vector, forces, energies):
    for b in range(2):
        cut = slice(b * 128, (b + 1) * 128)
        both = own[:, cut] + sent[dest[b]]
        forces[:, cut] = both[16:19]
        energies[:, cut] = (
            dot(read_vector[...], silu(both[0:16]), 1, 0, highest) + both[19:20]
        )


def whole(shape, dtype=f32):
    return jax.ShapeDtypeStruct(shape, dtype)


def blocks_of(shape):
    return pl.BlockSpec(shape, lambda i, home: (0,) * len(shape))


def on_device(
    positions,
    species,
    features,
    move_dest,
    move_slot,
    halo_list,
    neighbours,
    neighbour_count,
    wave_index,
    radial_in,
    radial_mid,
    radial_out,
    up_weight,
    prod_weight,
    out_weight,
    skip_weight,
    charge_weight,
    field_weight,
    read_weight,
    read_vector,
    force_weight,
):
    place = jnp.stack([lax.axis_index("gx"), lax.axis_index("yz")]).astype(i32)
    force_row = force_weight.reshape(1, 128)
    vmem = pl.BlockSpec(memory_space=pltpu.VMEM)

    read_rows = read_weight.T
    send_up, charges = pl.pallas_call(
        up_kernel,
        out_shape=(whole((2, 512, 128), bf16), whole((8, 256))),
        compiler_params=params(56),
        cost_estimate=cost(1 << 25, 0, 1 << 20),
        name="up",
    )(features, up_weight, charge_weight.T)
    moved_up = lax.all_gather(send_up, "yz", axis=0, tiled=True)

    moments, basis, waves = pl.pallas_call(
        moment_kernel,
        out_shape=(
            whole((128, 16, 128), bf16),
            whole((128 * SLABS, 512)),
            whole((40, 256)),
        ),
        in_specs=[SMEM] * 3 + [vmem] * 4,
        scratch_shapes=[pltpu.VMEM((128, 16, 128), f32)],
        compiler_params=params(56),
        cost_estimate=cost(1 << 30, 1 << 15, 3 << 20),
        name="moment",
    )(
        move_dest,
        move_slot,
        place,
        charges,
        positions,
        species.reshape(1, 256),
        halo_list.reshape(1, 32),
    )
    sent = lax.all_to_all(moments, ("gx", "yz"), 0, 0, tiled=True)
    coeffs = pl.pallas_call(
        weight_kernel,
        out_shape=whole((128, 8, 128)),
        in_specs=[SMEM, vmem, vmem],
        compiler_params=params(12),
        cost_estimate=cost(1 << 27, 1 << 11, 1 << 20),
        name="weight",
    )(place, sent, wave_index)
    coeffs = lax.all_to_all(coeffs, ("gx", "yz"), 0, 0, tiled=True)

    hidden, offsets, kinds, home = pl.pallas_call(
        radial_kernel,
        out_shape=(
            whole((64, 64, 256), bf16),
            whole((3, 64, 256)),
            whole((1, 256)),
            whole((2,), i32),
        ),
        in_specs=[SMEM] + [vmem] * 5,
        out_specs=(vmem, vmem, vmem, SMEM),
        scratch_shapes=[
            pltpu.VMEM((128, 16, 128), f32),
            pltpu.VMEM((64, 256), f32),
            pltpu.VMEM((64, 256), f32),
        ],
        compiler_params=params(16),
        cost_estimate=cost(1 << 32, 1 << 22, 4 << 20),
        name="radial",
    )(place, sent, neighbours.T, neighbour_count.reshape(1, 256), radial_in, radial_mid)

    nearby = [
        pl.BlockSpec((1, 512, 128), lambda i, home: (home[0], 0, 0)),
        pl.BlockSpec((1, 512, 128), lambda i, home: (home[1], 0, 0)),
    ]
    send_halo = pl.pallas_call(
        halo_kernel,
        out_shape=whole((32, 512), bf16),
        grid_spec=pltpu.PrefetchScalarGridSpec(
            num_scalar_prefetch=1,
            grid=(1,),
            in_specs=nearby + [blocks_of((1, 32))],
            out_specs=blocks_of((32, 512)),
        ),
        compiler_params=params(4),
        cost_estimate=cost(1 << 24, 0, 1 << 18),
        name="halo",
    )(home, moved_up, moved_up, halo_list.reshape(1, 32))
    ghosts = []
    for axis in ("gx", "yz"):
        count = lax.axis_size(axis)
        up = [(i, (i + 1) % count) for i in range(count)]
        ghosts.append(lax.ppermute(send_halo, axis, up))
        ghosts.append(lax.ppermute(send_halo, axis, [(b, a) for a, b in up]))

    part = pl.pallas_call(
        field_kernel,
        out_shape=whole((24, 256)),
        scratch_shapes=[pltpu.VMEM((384, 128 * SLABS), f32)],
        compiler_params=params(16),
        cost_estimate=cost(1 << 31, 0, 3 << 20),
        name="field",
    )(coeffs, basis, waves, features, skip_weight, field_weight, read_rows, force_row)

    returned = pl.pallas_call(
        message_kernel,
        out_shape=whole((16, 24, 128)),
        grid_spec=pltpu.PrefetchScalarGridSpec(
            num_scalar_prefetch=1,
            grid=(1,),
            in_specs=nearby
            + [blocks_of((32, 512))] * 4
            + [
                blocks_of((64, 256)),
                blocks_of((3, 64, 256)),
                blocks_of((64, 64, 256)),
                blocks_of((1, 256)),
                blocks_of((64, 512)),
                blocks_of((6, 640)),
                blocks_of((2, 128, 128)),
                blocks_of((16, 128)),
                blocks_of((1, 128)),
            ],
            out_specs=blocks_of((16, 24, 128)),
            scratch_shapes=[pltpu.VMEM((512, 384), bf16), pltpu.VMEM((512, 256), f32)],
        ),
        compiler_params=params(16),
        cost_estimate=cost(12 << 30, 0, 4 << 20),
        name="message",
    )(
        home,
        moved_up,
        moved_up,
        *ghosts,
        neighbours.T,
        offsets,
        hidden,
        kinds,
        radial_out,
        prod_weight,
        out_weight,
        read_rows,
        force_row,
    )
    returned = lax.all_to_all(returned, "yz", 0, 0, tiled=True)
    forces, energies = pl.pallas_call(
        final_kernel,
        out_shape=(whole((3, 256)), whole((1, 256))),
        in_specs=[SMEM, vmem, vmem, vmem],
        compiler_params=params(4),
        cost_estimate=cost(1 << 14, 1 << 12, 1 << 16),
        name="final",
    )(move_dest, returned, part, read_vector.reshape(1, 16))
    return forces, energies.reshape(256)


def solution(mesh):
    whole_spec = P(("gx", "yz"))
    in_specs = (
        (P(None, ("gx", "yz")), whole_spec, P(("gx", "yz"), None))
        + (whole_spec,) * 3
        + (P(("gx", "yz"), None), whole_spec)
        + (P(),) * 13
    )
    out_specs = (P(None, ("gx", "yz")), whole_spec)
    return jax.shard_map(
        on_device, mesh=mesh, in_specs=in_specs, out_specs=out_specs, check_vma=False
    )
```

```python
import math

import jax
import jax.numpy as jnp
from jax import lax
from jax.experimental import pallas as pl
from jax.experimental.pallas import tpu as pltpu
from jax.sharding import PartitionSpec as P

f32, bf16, i32 = jnp.float32, jnp.bfloat16, jnp.int32
highest = lax.Precision.HIGHEST
two_pi = 2.0 * math.pi
cutoff_radius = 3.5
ewald_width = 0.1
ewald_scale = 0.01

NX, NY, NZ = 16, 32, 2
SLABS = 2 * NZ + 2
RADIAL_GROUP, SLOT_GROUP = 16, 8


def row_of(chunk, component):
    return 128 * chunk + 32 * component


def dot(a, b, ca, cb, precision=None):
    return lax.dot_general(
        a, b, (((ca,), (cb,)), ((), ())), precision=precision, preferred_element_type=f32
    )


def halves(v):
    high = v.astype(bf16)
    return high, (v - high.astype(f32)).astype(bf16)


def dot_halves(a, b, ca, cb):
    return dot(a[0], b[0], ca, cb) + (dot(a[0], b[1], ca, cb) + dot(a[1], b[0], ca, cb))


def silu(v):
    half = 0.5 * v
    return half + half * jnp.tanh(half)


def iota(shape, dim):
    return lax.broadcasted_iota(i32, shape, dim)


def turns(t):
    angle = two_pi * (t - jnp.floor(t + 0.5))
    return jnp.cos(angle), jnp.sin(angle)


def params(mebibytes=58):
    return pltpu.CompilerParams(vmem_limit_bytes=mebibytes << 20)


def cost(flops, transcendentals, moved):
    return pl.CostEstimate(flops=flops, transcendentals=transcendentals, bytes_accessed=moved)


SMEM = pl.BlockSpec(memory_space=pltpu.SMEM)


def up_kernel(feat, up, charge_weight, out, charges):
    charges[...] = dot(charge_weight[...], feat[:, 0:128], 1, 1)
    for b in range(2):
        for c in range(4):
            rows = feat[b * 128 : (b + 1) * 128, c * 128 : (c + 1) * 128]
            mapped = dot(up[min(c, 1)], rows, 0, 1).astype(bf16)
            for q in range(4):
                out[b, row_of(q, c) : row_of(q, c) + 32, :] = mapped[32 * q : 32 * (q + 1)]


def moment_kernel(
    dest, slot, place, charges_in, pos, species, halo, out, basis_high, basis_low, waves, basis, stage
):
    gx = place[0].astype(f32)
    charges = charges_in[...]
    lane = iota((1, 256), 1)
    second = lane >= 128
    xyz = pos[...].astype(f32)
    along_x = xyz[0:1] + gx
    along_y = xyz[1:2] + jnp.where(second, dest[1], dest[0]).astype(f32)
    along_z = xyz[2:3]
    cos_x, sin_x = turns((iota((NX, 256), 0) + 1).astype(f32) * along_x * (1.0 / 8.0))
    cos_y, sin_y = turns((iota((NY, 256), 0) + 1).astype(f32) * along_y * (1.0 / 16.0))
    cos_z, sin_z = turns(iota((8, 256), 0).astype(f32) * along_z)
    pairs = [
        (cos_z[abs(z) : abs(z) + 1], sin_z[abs(z) : abs(z) + 1] * (1.0 if z >= 0 else -1.0))
        for z in range(-NZ, NZ + 1)
    ]
    for i, (c, s) in enumerate(pairs):
        at = i * 128
        basis[at : at + 32, 0:256] = cos_y * c
        basis[at + 32 : at + 64, 0:256] = sin_y * c
        basis[at + 64 : at + 96, 0:256] = cos_y * s
        basis[at + 96 : at + 128, 0:256] = sin_y * s
        basis[at : at + 32, 256:512] = -(cos_y * s)
        basis[at + 32 : at + 64, 256:512] = -(sin_y * s)
        basis[at + 64 : at + 96, 256:512] = cos_y * c
        basis[at + 96 : at + 128, 256:512] = sin_y * c
    at = 128 * (SLABS - 1)
    basis[at : at + 128, :] = jnp.zeros((128, 512), f32)
    for i, (c, s) in enumerate(pairs):
        basis[at + i : at + i + 1, 0:256] = c
        basis[at + i : at + i + 1, 256:512] = -s
        basis[at + 64 + i : at + 65 + i, 0:256] = s
        basis[at + 64 + i : at + 65 + i, 256:512] = c
    waves[0:8] = charges
    waves[8:24] = cos_x
    waves[24:40] = sin_x
    left_cos = (cos_x[:, None, :] * charges[None]).reshape(128, 256)
    left_sin = (sin_x[:, None, :] * charges[None]).reshape(128, 256)
    basis_high[...], basis_low[...] = halves(basis[...])
    left = halves(jnp.concatenate([left_cos, left_sin], axis=1))
    moments = dot_halves(left, (basis_high[...], basis_low[...]), 1, 1)
    for i in range(SLABS):
        stage[:, i, :] = moments[:, i * 128 : (i + 1) * 128]
    kinds = species[...].astype(f32)
    for b in range(2):
        cut = slice(b * 128, (b + 1) * 128)
        for m in range(3):
            stage[:, 6 + 3 * b + m, :] = jnp.broadcast_to(xyz[m : m + 1, cut], (128, 128))
        stage[:, 12 + b, :] = jnp.broadcast_to(kinds[:, cut], (128, 128))
    listed = jnp.concatenate([halo[...], jnp.zeros((1, 96), i32)], axis=1)
    at = iota((1, 128), 1)
    for b in range(2):
        listed = jnp.where(at == 32 + b, dest[b], listed)
        listed = jnp.where(at == 34 + b, slot[b], listed)
    stage[:, 14, :] = jnp.broadcast_to(listed.astype(f32), (128, 128))
    stage[:, 15, :] = jnp.zeros((128, 128), f32)
    out[...] = stage[...].astype(bf16)


def count_kernel(place, wave_index, out):
    own_x = (place[0] * 16 + place[1]) // 8 + 1
    kx, ky, kz = wave_index[0:1, :], wave_index[1:2, :], wave_index[2:3, :]
    count = kx.shape[1]
    ours = kx == own_x
    rank = iota((8, count), 0)
    z_rows = jnp.where(ours & (kz == rank - NZ), 1.0, 0.0).astype(bf16)
    flat_rows = jnp.where(ours & (ky == 0) & (rank == SLABS - 1), 1.0, 0.0).astype(bf16)
    z_any = jnp.where(kz == rank - NZ, 1.0, 0.0).astype(bf16)
    y_match = jnp.where(jnp.abs(ky) == iota((NY, count), 0) + 1, 1.0, 0.0)
    y_sign = jnp.where(ky < 0, -y_match, y_match)
    even = dot(z_rows, y_match.astype(bf16), 1, 1)
    odd = dot(z_rows, y_sign.astype(bf16), 1, 1)
    flat = dot(flat_rows, z_any, 1, 1)
    gap = jnp.zeros((8, 56), f32)
    even = jnp.concatenate([even] * 4, axis=1)
    odd = jnp.concatenate([odd] * 4, axis=1)
    flat = jnp.concatenate([flat, gap] * 2, axis=1)
    row, lane = iota((8, 128), 0), iota((8, 128), 1)
    in_flat = row == SLABS - 1
    x_wave = own_x.astype(f32) * (two_pi / 8.0)
    y_wave = jnp.where(in_flat, 0, lane % 32 + 1).astype(f32) * (two_pi / 16.0)
    z_wave = (jnp.where(in_flat, lane % 64, row) - NZ).astype(f32) * two_pi
    squared = x_wave * x_wave + y_wave * y_wave + z_wave * z_wave
    prefactor = 8.0 * math.pi * ewald_scale / 128.0
    weight = prefactor * jnp.exp(-0.5 * ewald_width * ewald_width * squared) / squared
    out[0:8] = weight * jnp.where(in_flat, flat, even)
    out[8:16] = weight * jnp.where(in_flat, 0.0, odd)


def weight_kernel(
    place, sent, weights, out, table_out, kinds_out, lists_out, home_out, stage
):
    stage[...] = sent[...].astype(f32)
    total = jnp.sum(stage[:, 0:8, :], axis=0)
    row, lane = iota((8, 128), 0), iota((8, 128), 1)
    total = jnp.where(row < SLABS, total, 0.0)
    far = pltpu.roll(total, 64, 1)
    group = lane // 32
    swapped = jnp.where(group % 2 == 0, pltpu.roll(far, 96, 1), pltpu.roll(far, 32, 1))
    swapped = jnp.where((group == 0) | (group == 3), -swapped, swapped)
    coefficient = total * weights[0:8] + swapped * weights[8:16]
    out[...] = jnp.broadcast_to(coefficient[None], out.shape)
    gx, yz = place[0], place[1]
    targets = [
        (gx, yz),
        ((gx + 7) % 8, yz),
        ((gx + 1) % 8, yz),
        (gx, (yz + 15) % 16),
        (gx, (yz + 1) % 16),
    ]
    plan = jnp.transpose(stage[:, 14, :])
    row = iota((16, 128), 0)
    device = iota((16, 128), 1)
    want_x, want_y = jnp.full((16, 128), -1, i32), jnp.full((16, 128), -1, i32)
    for t, (tx, ty) in enumerate(targets):
        want_x = jnp.where(row // 2 == t, tx, want_x)
        want_y = jnp.where(row // 2 == t, ty, want_y)
    here = (device // 16 == want_x).astype(f32)
    want_y, want_slot = want_y.astype(f32), (row % 2).astype(f32)
    picks = []
    for b in range(2):
        match = (plan[32 + b : 33 + b] == want_y) & (plan[34 + b : 35 + b] == want_slot)
        picks.append(jnp.where(match, here, 0.0))
    exact = [pick.astype(bf16) for pick in picks]

    def from_home(first, step):
        return sum(
            dot(exact[b], stage[:, first + b * step, :].astype(bf16), 1, 0) for b in range(2)
        )

    xyz = [from_home(6 + m, 3) for m in range(3)]
    kinds = from_home(12, 1)
    kinds_out[...] = jnp.concatenate([kinds[0:1], kinds[1:2]], axis=1)
    both = picks[0] + picks[1]
    column = 2.0 * both * (device % 16).astype(f32) + picks[1]
    for i, r in enumerate((0, 1, 6, 7, 8, 9)):
        home_out[i] = jnp.sum(jnp.where(row == r, column, 0.0)).astype(i32)
    lane = iota((1, 128), 1)
    atom = iota((128, 128), 0)
    ghosts = jnp.zeros((8, 128), f32)
    for t, (tx, ty) in enumerate(targets[1:]):
        listed = stage[tx * 16 + ty, 14:15, :].astype(i32)
        if t:
            listed = pltpu.roll(listed, 32 * t, 1)
        listed = jnp.where(lane // 32 == t, listed, -1)
        lists_out[t : t + 1] = listed
        for s in range(2):
            at = 2 * (t + 1) + s
            rows = jnp.concatenate(
                [x[at : at + 1] for x in xyz] + [jnp.zeros((5, 128), f32)], axis=0
            )
            chosen = jnp.where(atom + 128 * s == listed, 1.0, 0.0).astype(bf16)
            ghosts = ghosts + dot(rows.astype(bf16), chosen, 1, 0)
    part = lane // 32
    shifts = [
        jnp.where(part == 0, -1.0, jnp.where(part == 1, 1.0, 0.0)),
        jnp.where(part == 2, -1.0, jnp.where(part == 3, 1.0, 0.0)),
        jnp.zeros((1, 128), f32),
    ]
    zero = jnp.zeros((1, 128), f32)
    rows = [v for m in range(3) for v in (xyz[m][0:1], xyz[m][1:2], ghosts[m : m + 1] + shifts[m])]
    table_out[...] = jnp.concatenate(rows + [zero] * 7, axis=0)


def field_kernel(
    coeffs,
    basis_high,
    basis_low,
    waves,
    feat,
    skip_weight,
    field_weight,
    read_weight,
    force_weight,
    out,
    stacked,
):
    lane = iota((128, 128), 1)
    group_even = (lane // 32) % 2 == 0
    low_half = lane < 64
    y_wave = (lane % 32 + 1).astype(f32) * (two_pi / 16.0)
    for i in range(SLABS):
        cut = slice(i * 128, (i + 1) * 128)
        c = coeffs[:, i, :]
        stacked[0:128, cut] = c
        half = pltpu.roll(c, 64, 1)
        if i < SLABS - 1:
            moved = jnp.where(group_even, pltpu.roll(c, 96, 1), -pltpu.roll(c, 32, 1))
            stacked[128:256, cut] = y_wave * moved
            z_wave = two_pi * (i - NZ)
        else:
            stacked[128:256, cut] = jnp.zeros((128, 128), f32)
            z_wave = (lane % 64 - NZ).astype(f32) * two_pi
        stacked[256:384, cut] = z_wave * jnp.where(low_half, half, -half)
    grid = dot_halves(halves(stacked[...]), (basis_high[...], basis_low[...]), 1, 0)
    charges = waves[0:8]
    cos_x = jnp.broadcast_to(waves[8:24][:, None, :], (NX, 8, 256)).reshape(128, 256)
    sin_x = jnp.broadcast_to(waves[24:40][:, None, :], (NX, 8, 256)).reshape(128, 256)
    x_wave = (iota((128, 256), 0) // 8 + 1).astype(f32) * (two_pi / 8.0)

    def channels(v):
        return jnp.sum(v.reshape(NX, 8, 256), axis=0)

    def even_part(at):
        return channels(cos_x * grid[at : at + 128, 0:256] + sin_x * grid[at : at + 128, 256:512])

    potential = even_part(0)
    field = [
        channels(x_wave * (sin_x * grid[0:128, 0:256] - cos_x * grid[0:128, 256:512])),
        -even_part(128),
        -even_part(256),
    ]
    scalars = dot(field_weight[...], potential, 0, 0, highest) + dot(
        skip_weight[0], feat[:, 0:128], 0, 1
    )
    out[0:16] = dot(read_weight[...].astype(f32), scalars, 1, 0, highest)
    for m in range(3):
        vector = dot(skip_weight[1], feat[:, (m + 1) * 128 : (m + 2) * 128], 0, 1)
        out[16 + m : 17 + m] = dot(force_weight[...], vector, 1, 0, highest) + jnp.sum(
            charges * field[m], axis=0, keepdims=True
        )
    out[19:20] = 0.5 * jnp.sum(charges * potential, axis=0, keepdims=True)
    out[20:24] = jnp.zeros((4, 256), f32)


def radial_kernel(
    table,
    neighbours,
    live,
    radial_in,
    radial_mid,
    hidden_out,
    offset_out,
    dist_stage,
    scale_stage,
):
    tables = [
        [jnp.broadcast_to(table[3 * m + i : 3 * m + i + 1], (8, 128)) for i in range(3)]
        for m in range(3)
    ]
    for n in range(0, 64, 8):
        for half in range(2):
            cut = slice(half * 128, (half + 1) * 128)
            index = neighbours[n : n + 8, cut]
            within, block = index & 127, index >> 7
            squared = jnp.zeros((8, 128), f32)
            for m in range(3):
                found = [
                    jnp.take_along_axis(table, within, axis=1, mode="promise_in_bounds")
                    for table in tables[m]
                ]
                picked = jnp.where(block == 0, found[0], jnp.where(block == 1, found[1], found[2]))
                offset = picked - tables[m][half]
                offset_out[m, n : n + 8, cut] = offset
                squared = squared + offset * offset
            dist = jnp.sqrt(squared)
            dist_stage[n : n + 8, cut] = dist
            u = dist * (1.0 / cutoff_radius)
            u6 = (u * u) * (u * u) * (u * u)
            envelope = 1.0 + u6 * (-28.0 + u * (48.0 - 21.0 * u))
            alive = iota((8, 128), 0) + n < live[:, cut]
            scale_stage[n : n + 8, cut] = jnp.where(alive, 0.125 * envelope, 0.0)
    first = jnp.transpose(radial_in[...].astype(f32)).astype(bf16)
    mid = [jnp.transpose(radial_mid[i].astype(f32)).astype(bf16) for i in range(2)]
    centre = iota((8, 256), 0).astype(f32) * (cutoff_radius / 7.0)

    def body(group, carry):
        start = group * RADIAL_GROUP
        rows = []
        for j in range(RADIAL_GROUP):
            away = dist_stage[pl.ds(start + j, 1), :] - centre
            rows.append(jnp.exp(-4.0 * (away * away)))
        hidden = silu(dot(first, jnp.concatenate(rows, axis=1).astype(bf16), 1, 0)).astype(bf16)
        hidden = silu(dot(mid[0], hidden, 1, 0)).astype(bf16)
        hidden = silu(dot(mid[1], hidden, 1, 0))
        for j in range(RADIAL_GROUP):
            scaled = hidden[:, j * 256 : (j + 1) * 256] * scale_stage[pl.ds(start + j, 1), :]
            hidden_out[start + j] = scaled.astype(bf16)
        return carry

    lax.fori_loop(0, 64 // RADIAL_GROUP, body, 0)


def spread_kernel(hidden, radial_out, out, spread):
    mapped = jnp.transpose(radial_out[...].astype(f32)).astype(bf16)
    for q in range(4):
        for c in range(4):
            at = 128 * c + 32 * q
            spread[row_of(q, c) : row_of(q, c) + 32] = mapped[at : at + 32]

    def body(group, carry):
        for j in range(SLOT_GROUP):
            n = group * SLOT_GROUP + j
            out[n] = dot(spread[...], hidden[n], 1, 0).astype(bf16)
        return carry

    lax.fori_loop(0, 64 // SLOT_GROUP, body, 0)


def near_kernel(home, own0, own1, low0, low1, high0, high1, lists, table):
    table[:, 0:128] = own0[0]
    table[:, 128:256] = own1[0]
    atom = iota((128, 128), 0)
    ghosts = jnp.zeros((512, 128), f32)
    for t, pair in ((2, (low0, low1)), (3, (high0, high1))):
        for s, block in enumerate(pair):
            chosen = jnp.where(atom + 128 * s == lists[t : t + 1], 1.0, 0.0).astype(bf16)
            ghosts = ghosts + dot(block[0], chosen, 1, 0)
    table[:, 256:384] = ghosts.astype(bf16)


def halo_kernel(home, first, second, halo, out):
    atom = iota((128, 32), 0)
    chosen = [jnp.where(atom + 128 * s == halo[...], 1.0, 0.0).astype(bf16) for s in range(2)]
    out[...] = (dot(chosen[0], first[0], 0, 1) + dot(chosen[1], second[0], 0, 1)).astype(bf16)


def message_kernel(
    home,
    near,
    left,
    right,
    neighbours,
    offsets,
    radials,
    kinds,
    prod_weight,
    out_weight,
    read_weight,
    force_weight,
    out,
    table,
    total,
):
    table[...] = near[...]
    table[:, 256:288] = jnp.transpose(left[...].astype(f32)).astype(bf16)
    table[:, 288:320] = jnp.transpose(right[...].astype(f32)).astype(bf16)
    total[...] = jnp.zeros((512, 256), f32)
    own_place = iota((256, 256), 0).astype(f32).astype(bf16)
    ghost_place = iota((128, 256), 0).astype(f32).astype(bf16)

    def choice(n):
        row = neighbours[pl.ds(n, 1), :]
        own = jnp.where(row < 256, row, -1).astype(f32).astype(bf16)
        ghost = (row - 256).astype(f32).astype(bf16)
        one, none = jnp.ones((), bf16), jnp.zeros((), bf16)
        return jnp.concatenate(
            [jnp.where(own_place == own, one, none), jnp.where(ghost_place == ghost, one, none)],
            axis=0,
        )

    def body(group, carry):
        slots = [group * SLOT_GROUP + j for j in range(SLOT_GROUP)]
        chosen = [choice(n) for n in slots]
        away = [[offsets[m, pl.ds(n, 1), :] for m in range(3)] for n in slots]
        for q in range(4):
            rows = slice(128 * q, 128 * (q + 1))
            cuts = [slice(row_of(q, c), row_of(q, c) + 32) for c in range(4)]
            sums = [total[cut] for cut in cuts]
            for j, r in enumerate(away):
                up = dot(table[rows], chosen[j], 1, 0)
                radial = radials[slots[j], rows].astype(f32)
                u = [up[32 * c : 32 * (c + 1)] for c in range(4)]
                path = [radial[32 * c : 32 * (c + 1)] for c in range(4)]
                along = u[1] * r[0] + u[2] * r[1] + u[3] * r[2]
                sums[0] = sums[0] + path[0] * u[0] + path[1] * along
                scalar = path[2] * u[0]
                for m in range(3):
                    sums[m + 1] = sums[m + 1] + scalar * r[m] + path[3] * u[m + 1]
            for cut, value in zip(cuts, sums):
                total[cut] = value
        return carry

    lax.fori_loop(0, 64 // SLOT_GROUP, body, 0)
    finish_messages(total, home, kinds, prod_weight, out_weight, read_weight, force_weight, out)


def finish_messages(
    total, home, kinds, prod_weight, out_weight, read_weight, force_weight, out
):
    kind = jnp.where(iota((6, 256), 0).astype(f32) == kinds[...], 1.0, 0.0)
    paths = dot(prod_weight[...], kind, 0, 0, highest)
    p = [paths[128 * i : 128 * (i + 1)] for i in range(5)]
    a0, *a1 = [
        jnp.concatenate([total[row_of(q, c) : row_of(q, c) + 32] for q in range(4)], axis=0)
        for c in range(4)
    ]
    square = a1[0] * a1[0] + a1[1] * a1[1] + a1[2] * a1[2]
    b0 = (p[0] * a0 + p[1] * a0 * a0 + p[2] * square).astype(bf16)
    rows = [dot(read_weight[...].astype(f32), dot(out_weight[0], b0, 0, 0), 1, 0, highest)]
    for m in range(3):
        b1 = (p[3] * a1[m] + p[4] * a0 * a1[m]).astype(bf16)
        rows.append(dot(force_weight[...], dot(out_weight[1], b1, 0, 0), 1, 0, highest))
    rows.append(jnp.zeros((5, 256), f32))
    result = jnp.concatenate(rows, axis=0)
    out[...] = jnp.zeros(out.shape, f32)
    for s in range(2):
        out[home[s] // 2] = result[:, s * 128 : (s + 1) * 128]


def final_kernel(dest, sent, own, read_vector, forces, energies):
    for b in range(2):
        cut = slice(b * 128, (b + 1) * 128)
        both = own[:, cut] + sent[dest[b]]
        forces[:, cut] = both[16:19]
        energies[:, cut] = (
            dot(read_vector[...], silu(both[0:16]), 1, 0, highest) + both[19:20]
        )


def whole(shape, dtype=f32):
    return jax.ShapeDtypeStruct(shape, dtype)


def blocks_of(shape):
    return pl.BlockSpec(shape, lambda i, home: (0,) * len(shape))


def on_device(
    positions,
    species,
    features,
    move_dest,
    move_slot,
    halo_list,
    neighbours,
    neighbour_count,
    wave_index,
    radial_in,
    radial_mid,
    radial_out,
    up_weight,
    prod_weight,
    out_weight,
    skip_weight,
    charge_weight,
    field_weight,
    read_weight,
    read_vector,
    force_weight,
):
    place = jnp.stack([lax.axis_index("gx"), lax.axis_index("yz")]).astype(i32)
    force_row = force_weight.reshape(1, 128)
    vmem = pl.BlockSpec(memory_space=pltpu.VMEM)

    read_rows = read_weight.T
    send_up, charges = pl.pallas_call(
        up_kernel,
        out_shape=(whole((2, 512, 128), bf16), whole((8, 256))),
        compiler_params=params(),
        cost_estimate=cost(1 << 25, 0, 1 << 20),
        name="up",
    )(features, up_weight, charge_weight.T)
    moved_up = lax.all_gather(send_up, "yz", axis=0, tiled=True)

    moments, basis_high, basis_low, waves = pl.pallas_call(
        moment_kernel,
        out_shape=(
            whole((128, 16, 128), bf16),
            whole((128 * SLABS, 512), bf16),
            whole((128 * SLABS, 512), bf16),
            whole((40, 256)),
        ),
        in_specs=[SMEM] * 3 + [vmem] * 4,
        scratch_shapes=[
            pltpu.VMEM((128 * SLABS, 512), f32),
            pltpu.VMEM((128, 16, 128), f32),
        ],
        compiler_params=params(),
        cost_estimate=cost(1 << 30, 1 << 15, 3 << 20),
        name="moment",
    )(
        move_dest,
        move_slot,
        place,
        charges,
        positions,
        species.reshape(1, 256),
        halo_list.reshape(1, 32),
    )
    sent = lax.all_to_all(moments, ("gx", "yz"), 0, 0, tiled=True)
    weights = pl.pallas_call(
        count_kernel,
        out_shape=whole((16, 128)),
        in_specs=[SMEM, vmem],
        compiler_params=params(),
        cost_estimate=cost(1 << 28, 1 << 11, 1 << 18),
        name="count",
    )(place, wave_index)
    coeffs, table, kinds, lists, home = pl.pallas_call(
        weight_kernel,
        out_shape=(
            whole((128, 8, 128)),
            whole((16, 128)),
            whole((1, 256)),
            whole((4, 128), i32),
            whole((6,), i32),
        ),
        in_specs=[SMEM, vmem, vmem],
        out_specs=(vmem, vmem, vmem, vmem, SMEM),
        scratch_shapes=[pltpu.VMEM((128, 16, 128), f32)],
        compiler_params=params(),
        cost_estimate=cost(1 << 27, 1 << 11, 1 << 20),
        name="weight",
    )(place, sent, weights)
    coeffs = lax.all_to_all(coeffs, ("gx", "yz"), 0, 0, tiled=True)

    hidden, offsets = pl.pallas_call(
        radial_kernel,
        out_shape=(whole((64, 64, 256), bf16), whole((3, 64, 256))),
        scratch_shapes=[pltpu.VMEM((64, 256), f32), pltpu.VMEM((64, 256), f32)],
        compiler_params=params(),
        cost_estimate=cost(1 << 32, 1 << 22, 4 << 20),
        name="radial",
    )(table, neighbours.T, neighbour_count.reshape(1, 256), radial_in, radial_mid)

    moved_up, hidden = lax.optimization_barrier((moved_up, hidden))
    nearby = [
        pl.BlockSpec((1, 512, 128), lambda i, home, at=at: (home[at], 0, 0)) for at in range(6)
    ]
    send_halo = pl.pallas_call(
        halo_kernel,
        out_shape=whole((32, 512), bf16),
        grid_spec=pltpu.PrefetchScalarGridSpec(
            num_scalar_prefetch=1,
            grid=(1,),
            in_specs=nearby[0:2] + [blocks_of((1, 32))],
            out_specs=blocks_of((32, 512)),
        ),
        compiler_params=params(),
        cost_estimate=cost(1 << 24, 0, 1 << 18),
        name="halo",
    )(home, moved_up, moved_up, halo_list.reshape(1, 32))
    send_halo, late_hidden, late_up = lax.optimization_barrier((send_halo, hidden, moved_up))
    near = pl.pallas_call(
        near_kernel,
        out_shape=whole((512, 384), bf16),
        grid_spec=pltpu.PrefetchScalarGridSpec(
            num_scalar_prefetch=1,
            grid=(1,),
            in_specs=nearby + [blocks_of((4, 128))],
            out_specs=blocks_of((512, 384)),
        ),
        compiler_params=params(12),
        cost_estimate=cost(1 << 28, 0, 1 << 20),
        name="near",
    )(home, *[late_up] * 6, lists)
    radials = pl.pallas_call(
        spread_kernel,
        out_shape=whole((64, 512, 256), bf16),
        in_specs=[vmem, vmem],
        out_specs=vmem,
        scratch_shapes=[pltpu.VMEM((512, 64), bf16)],
        compiler_params=params(12),
        cost_estimate=cost(6 << 30, 0, 18 << 20),
        name="spread",
    )(late_hidden, radial_out)
    up = [(i, (i + 1) % 8) for i in range(8)]
    left = lax.ppermute(send_halo, "gx", up)
    right = lax.ppermute(send_halo, "gx", [(b, a) for a, b in up])

    part = pl.pallas_call(
        field_kernel,
        out_shape=whole((24, 256)),
        scratch_shapes=[pltpu.VMEM((384, 128 * SLABS), f32)],
        compiler_params=params(),
        cost_estimate=cost(1 << 31, 0, 3 << 20),
        name="field",
    )(coeffs, basis_high, basis_low, waves, features, skip_weight, field_weight, read_rows, force_row)

    returned = pl.pallas_call(
        message_kernel,
        out_shape=whole((16, 24, 128)),
        in_specs=[SMEM] + [vmem] * 11,
        out_specs=vmem,
        scratch_shapes=[pltpu.VMEM((512, 384), bf16), pltpu.VMEM((512, 256), f32)],
        compiler_params=params(12),
        cost_estimate=cost(12 << 30, 0, 4 << 20),
        name="message",
    )(
        home,
        near,
        left,
        right,
        neighbours.T,
        offsets,
        radials,
        kinds,
        prod_weight,
        out_weight,
        read_rows,
        force_row,
    )
    returned = lax.all_to_all(returned, "yz", 0, 0, tiled=True)
    forces, energies = pl.pallas_call(
        final_kernel,
        out_shape=(whole((3, 256)), whole((1, 256))),
        in_specs=[SMEM, vmem, vmem, vmem],
        compiler_params=params(),
        cost_estimate=cost(1 << 14, 1 << 12, 1 << 16),
        name="final",
    )(move_dest, returned, part, read_vector.reshape(1, 16))
    return forces, energies.reshape(256)


def solution(mesh):
    whole_spec = P(("gx", "yz"))
    in_specs = (
        (P(None, ("gx", "yz")), whole_spec, P(("gx", "yz"), None))
        + (whole_spec,) * 3
        + (P(("gx", "yz"), None), whole_spec)
        + (P(),) * 13
    )
    out_specs = (P(None, ("gx", "yz")), whole_spec)
    return jax.shard_map(
        on_device, mesh=mesh, in_specs=in_specs, out_specs=out_specs, check_vma=False
    )
```

```python
import math

import jax
import jax.numpy as jnp
from jax import lax
from jax.experimental import pallas as pl
from jax.experimental.pallas import tpu as pltpu
from jax.sharding import PartitionSpec as P

f32, bf16, i32 = jnp.float32, jnp.bfloat16, jnp.int32
highest = lax.Precision.HIGHEST
two_pi = 2.0 * math.pi
cutoff_radius = 3.5
ewald_width = 0.1
ewald_scale = 0.01

NX, NY, NZ = 16, 32, 2
SLABS = 2 * NZ + 2
RADIAL_GROUP, SLOT_GROUP = 16, 16


def row_of(chunk, component):
    return 128 * chunk + 32 * component


def dot(a, b, ca, cb, precision=None):
    return lax.dot_general(
        a, b, (((ca,), (cb,)), ((), ())), precision=precision, preferred_element_type=f32
    )


def halves(v):
    high = v.astype(bf16)
    return high, (v - high.astype(f32)).astype(bf16)


def dot_halves(a, b, ca, cb):
    return dot(a[0], b[0], ca, cb) + (dot(a[0], b[1], ca, cb) + dot(a[1], b[0], ca, cb))


def silu(v):
    half = 0.5 * v
    return half + half * jnp.tanh(half)


def iota(shape, dim):
    return lax.broadcasted_iota(i32, shape, dim)


def turns(t):
    angle = two_pi * (t - jnp.floor(t + 0.5))
    return jnp.cos(angle), jnp.sin(angle)


def params(mebibytes=58):
    return pltpu.CompilerParams(vmem_limit_bytes=mebibytes << 20)


def cost(flops, transcendentals, moved):
    return pl.CostEstimate(flops=flops, transcendentals=transcendentals, bytes_accessed=moved)


SMEM = pl.BlockSpec(memory_space=pltpu.SMEM)


def up_kernel(feat, up, charge_weight, out, charges):
    charges[...] = dot(charge_weight[...], feat[:, 0:128], 1, 1)
    for b in range(2):
        for c in range(4):
            rows = feat[b * 128 : (b + 1) * 128, c * 128 : (c + 1) * 128]
            mapped = dot(up[min(c, 1)], rows, 0, 1).astype(bf16)
            for q in range(4):
                out[b, row_of(q, c) : row_of(q, c) + 32, :] = mapped[32 * q : 32 * (q + 1)]


def moment_kernel(
    dest, slot, charges_in, pos, species, halo, out, basis_high, basis_low, waves, basis, stage
):
    gx = lax.axis_index("gx").astype(f32)
    charges = charges_in[...]
    lane = iota((1, 256), 1)
    second = lane >= 128
    xyz = pos[...].astype(f32)
    along_x = xyz[0:1] + gx
    along_y = xyz[1:2] + jnp.where(second, dest[1], dest[0]).astype(f32)
    along_z = xyz[2:3]
    cos_x, sin_x = turns((iota((NX, 256), 0) + 1).astype(f32) * along_x * (1.0 / 8.0))
    cos_y, sin_y = turns((iota((NY, 256), 0) + 1).astype(f32) * along_y * (1.0 / 16.0))
    cos_z, sin_z = turns(iota((8, 256), 0).astype(f32) * along_z)
    pairs = [
        (cos_z[abs(z) : abs(z) + 1], sin_z[abs(z) : abs(z) + 1] * (1.0 if z >= 0 else -1.0))
        for z in range(-NZ, NZ + 1)
    ]
    for i, (c, s) in enumerate(pairs):
        at = i * 128
        basis[at : at + 32, 0:256] = cos_y * c
        basis[at + 32 : at + 64, 0:256] = sin_y * c
        basis[at + 64 : at + 96, 0:256] = cos_y * s
        basis[at + 96 : at + 128, 0:256] = sin_y * s
        basis[at : at + 32, 256:512] = -(cos_y * s)
        basis[at + 32 : at + 64, 256:512] = -(sin_y * s)
        basis[at + 64 : at + 96, 256:512] = cos_y * c
        basis[at + 96 : at + 128, 256:512] = sin_y * c
    at = 128 * (SLABS - 1)
    basis[at : at + 128, :] = jnp.zeros((128, 512), f32)
    for i, (c, s) in enumerate(pairs):
        basis[at + i : at + i + 1, 0:256] = c
        basis[at + i : at + i + 1, 256:512] = -s
        basis[at + 64 + i : at + 65 + i, 0:256] = s
        basis[at + 64 + i : at + 65 + i, 256:512] = c
    waves[0:8] = charges
    waves[8:24] = cos_x
    waves[24:40] = sin_x
    left_cos = (cos_x[:, None, :] * charges[None]).reshape(128, 256)
    left_sin = (sin_x[:, None, :] * charges[None]).reshape(128, 256)
    basis_high[...], basis_low[...] = halves(basis[...])
    left = halves(jnp.concatenate([left_cos, left_sin], axis=1))
    moments = dot_halves(left, (basis_high[...], basis_low[...]), 1, 1)
    for i in range(SLABS):
        stage[:, i, :] = moments[:, i * 128 : (i + 1) * 128]
    kinds = species[...].astype(f32)
    for b in range(2):
        cut = slice(b * 128, (b + 1) * 128)
        for m in range(3):
            stage[:, 6 + 3 * b + m, :] = jnp.broadcast_to(xyz[m : m + 1, cut], (128, 128))
        stage[:, 12 + b, :] = jnp.broadcast_to(kinds[:, cut], (128, 128))
    listed = jnp.concatenate([halo[...], jnp.zeros((1, 96), i32)], axis=1)
    at = iota((1, 128), 1)
    for b in range(2):
        listed = jnp.where(at == 32 + b, dest[b], listed)
        listed = jnp.where(at == 34 + b, slot[b], listed)
    stage[:, 14, :] = jnp.broadcast_to(listed.astype(f32), (128, 128))
    stage[:, 15, :] = jnp.zeros((128, 128), f32)
    out[...] = stage[...].astype(bf16)


def count_kernel(wave_index, out):
    own_x = (lax.axis_index("gx") * 16 + lax.axis_index("yz")) // 8 + 1
    kx, ky, kz = wave_index[0:1, :], wave_index[1:2, :], wave_index[2:3, :]
    count = kx.shape[1]
    ours = kx == own_x
    rank = iota((8, count), 0)
    z_rows = jnp.where(ours & (kz == rank - NZ), 1.0, 0.0).astype(bf16)
    flat_rows = jnp.where(ours & (ky == 0) & (rank == SLABS - 1), 1.0, 0.0).astype(bf16)
    z_any = jnp.where(kz == rank - NZ, 1.0, 0.0).astype(bf16)
    y_match = jnp.where(jnp.abs(ky) == iota((NY, count), 0) + 1, 1.0, 0.0)
    y_sign = jnp.where(ky < 0, -y_match, y_match)
    even = dot(z_rows, y_match.astype(bf16), 1, 1)
    odd = dot(z_rows, y_sign.astype(bf16), 1, 1)
    flat = dot(flat_rows, z_any, 1, 1)
    gap = jnp.zeros((8, 56), f32)
    even = jnp.concatenate([even] * 4, axis=1)
    odd = jnp.concatenate([odd] * 4, axis=1)
    flat = jnp.concatenate([flat, gap] * 2, axis=1)
    row, lane = iota((8, 128), 0), iota((8, 128), 1)
    in_flat = row == SLABS - 1
    x_wave = own_x.astype(f32) * (two_pi / 8.0)
    y_wave = jnp.where(in_flat, 0, lane % 32 + 1).astype(f32) * (two_pi / 16.0)
    z_wave = (jnp.where(in_flat, lane % 64, row) - NZ).astype(f32) * two_pi
    squared = x_wave * x_wave + y_wave * y_wave + z_wave * z_wave
    prefactor = 8.0 * math.pi * ewald_scale / 128.0
    weight = prefactor * jnp.exp(-0.5 * ewald_width * ewald_width * squared) / squared
    out[0:8] = weight * jnp.where(in_flat, flat, even)
    out[8:16] = weight * jnp.where(in_flat, 0.0, odd)


def weight_kernel(
    sent, weights, out, table_out, kinds_out, lists_out, home_out, stage
):
    stage[...] = sent[...].astype(f32)
    total = jnp.sum(stage[:, 0:8, :], axis=0)
    row, lane = iota((8, 128), 0), iota((8, 128), 1)
    total = jnp.where(row < SLABS, total, 0.0)
    far = pltpu.roll(total, 64, 1)
    group = lane // 32
    swapped = jnp.where(group % 2 == 0, pltpu.roll(far, 96, 1), pltpu.roll(far, 32, 1))
    swapped = jnp.where((group == 0) | (group == 3), -swapped, swapped)
    coefficient = total * weights[0:8] + swapped * weights[8:16]
    out[...] = jnp.broadcast_to(coefficient[None], out.shape)
    gx, yz = lax.axis_index("gx"), lax.axis_index("yz")
    targets = [
        (gx, yz),
        ((gx + 7) % 8, yz),
        ((gx + 1) % 8, yz),
        (gx, (yz + 15) % 16),
        (gx, (yz + 1) % 16),
    ]
    plan = jnp.transpose(stage[:, 14, :])
    row = iota((16, 128), 0)
    device = iota((16, 128), 1)
    want_x, want_y = jnp.full((16, 128), -1, i32), jnp.full((16, 128), -1, i32)
    for t, (tx, ty) in enumerate(targets):
        want_x = jnp.where(row // 2 == t, tx, want_x)
        want_y = jnp.where(row // 2 == t, ty, want_y)
    here = (device // 16 == want_x).astype(f32)
    want_y, want_slot = want_y.astype(f32), (row % 2).astype(f32)
    picks = []
    for b in range(2):
        match = (plan[32 + b : 33 + b] == want_y) & (plan[34 + b : 35 + b] == want_slot)
        picks.append(jnp.where(match, here, 0.0))
    exact = [pick.astype(bf16) for pick in picks]

    def from_home(first, step):
        return sum(
            dot(exact[b], stage[:, first + b * step, :].astype(bf16), 1, 0) for b in range(2)
        )

    xyz = [from_home(6 + m, 3) for m in range(3)]
    kinds = from_home(12, 1)
    kinds_out[...] = jnp.concatenate([kinds[0:1], kinds[1:2]], axis=1)
    both = picks[0] + picks[1]
    column = 2.0 * both * (device % 16).astype(f32) + picks[1]
    for i, r in enumerate((0, 1, 6, 7, 8, 9)):
        home_out[i] = jnp.sum(jnp.where(row == r, column, 0.0)).astype(i32)
    lane = iota((1, 128), 1)
    atom = iota((128, 128), 0)
    ghosts = jnp.zeros((8, 128), f32)
    for t, (tx, ty) in enumerate(targets[1:]):
        listed = stage[tx * 16 + ty, 14:15, :].astype(i32)
        if t:
            listed = pltpu.roll(listed, 32 * t, 1)
        listed = jnp.where(lane // 32 == t, listed, -1)
        lists_out[t : t + 1] = listed
        for s in range(2):
            at = 2 * (t + 1) + s
            rows = jnp.concatenate(
                [x[at : at + 1] for x in xyz] + [jnp.zeros((5, 128), f32)], axis=0
            )
            chosen = jnp.where(atom + 128 * s == listed, 1.0, 0.0).astype(bf16)
            ghosts = ghosts + dot(rows.astype(bf16), chosen, 1, 0)
    part = lane // 32
    shifts = [
        jnp.where(part == 0, -1.0, jnp.where(part == 1, 1.0, 0.0)),
        jnp.where(part == 2, -1.0, jnp.where(part == 3, 1.0, 0.0)),
        jnp.zeros((1, 128), f32),
    ]
    zero = jnp.zeros((1, 128), f32)
    rows = [v for m in range(3) for v in (xyz[m][0:1], xyz[m][1:2], ghosts[m : m + 1] + shifts[m])]
    table_out[...] = jnp.concatenate(rows + [zero] * 7, axis=0)


def field_kernel(
    coeffs,
    basis_high,
    basis_low,
    waves,
    feat,
    skip_weight,
    field_weight,
    read_weight,
    force_weight,
    out,
    stacked,
):
    lane = iota((128, 128), 1)
    group_even = (lane // 32) % 2 == 0
    low_half = lane < 64
    y_wave = (lane % 32 + 1).astype(f32) * (two_pi / 16.0)
    for i in range(SLABS):
        cut = slice(i * 128, (i + 1) * 128)
        c = coeffs[:, i, :]
        stacked[0:128, cut] = c
        half = pltpu.roll(c, 64, 1)
        if i < SLABS - 1:
            moved = jnp.where(group_even, pltpu.roll(c, 96, 1), -pltpu.roll(c, 32, 1))
            stacked[128:256, cut] = y_wave * moved
            z_wave = two_pi * (i - NZ)
        else:
            stacked[128:256, cut] = jnp.zeros((128, 128), f32)
            z_wave = (lane % 64 - NZ).astype(f32) * two_pi
        stacked[256:384, cut] = z_wave * jnp.where(low_half, half, -half)
    grid = dot_halves(halves(stacked[...]), (basis_high[...], basis_low[...]), 1, 0)
    charges = waves[0:8]
    cos_x = jnp.broadcast_to(waves[8:24][:, None, :], (NX, 8, 256)).reshape(128, 256)
    sin_x = jnp.broadcast_to(waves[24:40][:, None, :], (NX, 8, 256)).reshape(128, 256)
    x_wave = (iota((128, 256), 0) // 8 + 1).astype(f32) * (two_pi / 8.0)

    def channels(v):
        return jnp.sum(v.reshape(NX, 8, 256), axis=0)

    def even_part(at):
        return channels(cos_x * grid[at : at + 128, 0:256] + sin_x * grid[at : at + 128, 256:512])

    potential = even_part(0)
    field = [
        channels(x_wave * (sin_x * grid[0:128, 0:256] - cos_x * grid[0:128, 256:512])),
        -even_part(128),
        -even_part(256),
    ]
    scalars = dot(field_weight[...], potential, 0, 0, highest) + dot(
        skip_weight[0], feat[:, 0:128], 0, 1
    )
    out[0:16] = dot(read_weight[...].astype(f32), scalars, 1, 0, highest)
    for m in range(3):
        vector = dot(skip_weight[1], feat[:, (m + 1) * 128 : (m + 2) * 128], 0, 1)
        out[16 + m : 17 + m] = dot(force_weight[...], vector, 1, 0, highest) + jnp.sum(
            charges * field[m], axis=0, keepdims=True
        )
    out[19:20] = 0.5 * jnp.sum(charges * potential, axis=0, keepdims=True)
    out[20:24] = jnp.zeros((4, 256), f32)


def radial_kernel(
    table,
    neighbours,
    live,
    radial_in,
    radial_mid,
    hidden_out,
    offset_out,
    dist_stage,
    scale_stage,
):
    tables = [
        [jnp.broadcast_to(table[3 * m + i : 3 * m + i + 1], (8, 128)) for i in range(3)]
        for m in range(3)
    ]
    for n in range(0, 64, 8):
        for half in range(2):
            cut = slice(half * 128, (half + 1) * 128)
            index = neighbours[n : n + 8, cut]
            within, block = index & 127, index >> 7
            squared = jnp.zeros((8, 128), f32)
            for m in range(3):
                found = [
                    jnp.take_along_axis(table, within, axis=1, mode="promise_in_bounds")
                    for table in tables[m]
                ]
                picked = jnp.where(block == 0, found[0], jnp.where(block == 1, found[1], found[2]))
                offset = picked - tables[m][half]
                offset_out[m, n : n + 8, cut] = offset
                squared = squared + offset * offset
            dist = jnp.sqrt(squared)
            dist_stage[n : n + 8, cut] = dist
            u = dist * (1.0 / cutoff_radius)
            u6 = (u * u) * (u * u) * (u * u)
            envelope = 1.0 + u6 * (-28.0 + u * (48.0 - 21.0 * u))
            alive = iota((8, 128), 0) + n < live[:, cut]
            scale_stage[n : n + 8, cut] = jnp.where(alive, 0.125 * envelope, 0.0)
    first = jnp.transpose(radial_in[...].astype(f32)).astype(bf16)
    mid = [jnp.transpose(radial_mid[i].astype(f32)).astype(bf16) for i in range(2)]
    centre = iota((8, 256), 0).astype(f32) * (cutoff_radius / 7.0)

    def body(group, carry):
        start = group * RADIAL_GROUP
        rows = []
        for j in range(RADIAL_GROUP):
            away = dist_stage[pl.ds(start + j, 1), :] - centre
            rows.append(jnp.exp(-4.0 * (away * away)))
        hidden = silu(dot(first, jnp.concatenate(rows, axis=1).astype(bf16), 1, 0)).astype(bf16)
        hidden = silu(dot(mid[0], hidden, 1, 0)).astype(bf16)
        hidden = silu(dot(mid[1], hidden, 1, 0))
        for j in range(RADIAL_GROUP):
            scaled = hidden[:, j * 256 : (j + 1) * 256] * scale_stage[pl.ds(start + j, 1), :]
            hidden_out[start + j] = scaled.astype(bf16)
        return carry

    lax.fori_loop(0, 64 // RADIAL_GROUP, body, 0)


def spread_kernel(hidden, radial_out, out, spread):
    mapped = jnp.transpose(radial_out[...].astype(f32)).astype(bf16)
    for q in range(4):
        for c in range(4):
            at = 128 * c + 32 * q
            spread[row_of(q, c) : row_of(q, c) + 32] = mapped[at : at + 32]

    def body(group, carry):
        for j in range(SLOT_GROUP):
            n = group * SLOT_GROUP + j
            out[n] = dot(spread[...], hidden[n], 1, 0).astype(bf16)
        return carry

    lax.fori_loop(0, 64 // SLOT_GROUP, body, 0)


def near_kernel(home, own0, own1, low0, low1, high0, high1, lists, table):
    table[:, 0:128] = own0[0]
    table[:, 128:256] = own1[0]
    atom = iota((128, 128), 0)
    ghosts = jnp.zeros((512, 128), f32)
    for t, pair in ((2, (low0, low1)), (3, (high0, high1))):
        for s, block in enumerate(pair):
            chosen = jnp.where(atom + 128 * s == lists[t : t + 1], 1.0, 0.0).astype(bf16)
            ghosts = ghosts + dot(block[0], chosen, 1, 0)
    table[:, 256:384] = ghosts.astype(bf16)


def halo_kernel(home, first, second, halo, out):
    atom = iota((128, 32), 0)
    chosen = [jnp.where(atom + 128 * s == halo[...], 1.0, 0.0).astype(bf16) for s in range(2)]
    out[...] = (dot(chosen[0], first[0], 0, 1) + dot(chosen[1], second[0], 0, 1)).astype(bf16)


def message_kernel(
    home,
    near,
    left,
    right,
    neighbours,
    offsets,
    radials,
    kinds,
    prod_weight,
    out_weight,
    read_weight,
    force_weight,
    out,
    table,
    total,
):
    table[...] = near[...]
    table[:, 256:288] = jnp.transpose(left[...].astype(f32)).astype(bf16)
    table[:, 288:320] = jnp.transpose(right[...].astype(f32)).astype(bf16)
    total[...] = jnp.zeros((512, 256), f32)
    own_place = iota((256, 256), 0).astype(f32).astype(bf16)
    ghost_place = iota((128, 256), 0).astype(f32).astype(bf16)

    def choice(n):
        row = neighbours[pl.ds(n, 1), :]
        own = jnp.where(row < 256, row, -1).astype(f32).astype(bf16)
        ghost = (row - 256).astype(f32).astype(bf16)
        one, none = jnp.ones((), bf16), jnp.zeros((), bf16)
        return jnp.concatenate(
            [jnp.where(own_place == own, one, none), jnp.where(ghost_place == ghost, one, none)],
            axis=0,
        )

    def body(group, carry):
        slots = [group * SLOT_GROUP + j for j in range(SLOT_GROUP)]
        chosen = [choice(n) for n in slots]
        away = [[offsets[m, pl.ds(n, 1), :] for m in range(3)] for n in slots]
        for q in range(4):
            rows = slice(128 * q, 128 * (q + 1))
            cuts = [slice(row_of(q, c), row_of(q, c) + 32) for c in range(4)]
            sums = [total[cut] for cut in cuts]
            for j, r in enumerate(away):
                up = dot(table[rows], chosen[j], 1, 0)
                radial = radials[slots[j], rows].astype(f32)
                u = [up[32 * c : 32 * (c + 1)] for c in range(4)]
                path = [radial[32 * c : 32 * (c + 1)] for c in range(4)]
                along = u[1] * r[0] + u[2] * r[1] + u[3] * r[2]
                sums[0] = sums[0] + path[0] * u[0] + path[1] * along
                scalar = path[2] * u[0]
                for m in range(3):
                    sums[m + 1] = sums[m + 1] + scalar * r[m] + path[3] * u[m + 1]
            for cut, value in zip(cuts, sums):
                total[cut] = value
        return carry

    lax.fori_loop(0, 64 // SLOT_GROUP, body, 0)
    finish_messages(total, home, kinds, prod_weight, out_weight, read_weight, force_weight, out)


def finish_messages(
    total, home, kinds, prod_weight, out_weight, read_weight, force_weight, out
):
    kind = jnp.where(iota((6, 256), 0).astype(f32) == kinds[...], 1.0, 0.0)
    high, mid = halves(prod_weight[...])
    low = (prod_weight[...] - high.astype(f32) - mid.astype(f32)).astype(bf16)
    kind = kind.astype(bf16)
    paths = dot(high, kind, 0, 0) + (dot(mid, kind, 0, 0) + dot(low, kind, 0, 0))
    p = [paths[128 * i : 128 * (i + 1)] for i in range(5)]
    a0, *a1 = [
        jnp.concatenate([total[row_of(q, c) : row_of(q, c) + 32] for q in range(4)], axis=0)
        for c in range(4)
    ]
    square = a1[0] * a1[0] + a1[1] * a1[1] + a1[2] * a1[2]
    b0 = (p[0] * a0 + p[1] * a0 * a0 + p[2] * square).astype(bf16)
    rows = [dot(read_weight[...].astype(f32), dot(out_weight[0], b0, 0, 0), 1, 0, highest)]
    for m in range(3):
        b1 = (p[3] * a1[m] + p[4] * a0 * a1[m]).astype(bf16)
        rows.append(dot(force_weight[...], dot(out_weight[1], b1, 0, 0), 1, 0, highest))
    rows.append(jnp.zeros((5, 256), f32))
    result = jnp.concatenate(rows, axis=0)
    out[...] = jnp.zeros(out.shape, f32)
    for s in range(2):
        out[home[s] // 2] = result[:, s * 128 : (s + 1) * 128]


def final_kernel(dest, sent, own, read_vector, forces, energies):
    for b in range(2):
        cut = slice(b * 128, (b + 1) * 128)
        both = own[:, cut] + sent[dest[b]]
        forces[:, cut] = both[16:19]
        energies[:, cut] = (
            dot(read_vector[...], silu(both[0:16]), 1, 0, highest) + both[19:20]
        )


def whole(shape, dtype=f32):
    return jax.ShapeDtypeStruct(shape, dtype)


def blocks_of(shape):
    return pl.BlockSpec(shape, lambda i, home: (0,) * len(shape))


def on_device(
    positions,
    species,
    features,
    move_dest,
    move_slot,
    halo_list,
    neighbours,
    neighbour_count,
    wave_index,
    radial_in,
    radial_mid,
    radial_out,
    up_weight,
    prod_weight,
    out_weight,
    skip_weight,
    charge_weight,
    field_weight,
    read_weight,
    read_vector,
    force_weight,
):
    force_row = force_weight.reshape(1, 128)
    vmem = pl.BlockSpec(memory_space=pltpu.VMEM)

    read_rows = read_weight.T
    send_up, charges = pl.pallas_call(
        up_kernel,
        out_shape=(whole((2, 512, 128), bf16), whole((8, 256))),
        compiler_params=params(),
        cost_estimate=cost(1 << 25, 0, 1 << 20),
        name="up",
    )(features, up_weight, charge_weight.T)
    moved_up = lax.all_gather(send_up, "yz", axis=0, tiled=True)

    moments, basis_high, basis_low, waves = pl.pallas_call(
        moment_kernel,
        out_shape=(
            whole((128, 16, 128), bf16),
            whole((128 * SLABS, 512), bf16),
            whole((128 * SLABS, 512), bf16),
            whole((40, 256)),
        ),
        in_specs=[SMEM] * 2 + [vmem] * 4,
        scratch_shapes=[
            pltpu.VMEM((128 * SLABS, 512), f32),
            pltpu.VMEM((128, 16, 128), f32),
        ],
        compiler_params=params(20),
        cost_estimate=cost(1 << 30, 1 << 15, 3 << 20),
        name="moment",
    )(
        move_dest,
        move_slot,
        charges,
        positions,
        species.reshape(1, 256),
        halo_list.reshape(1, 32),
    )
    sent = lax.all_to_all(moments, ("gx", "yz"), 0, 0, tiled=True)
    weights = pl.pallas_call(
        count_kernel,
        out_shape=whole((16, 128)),
        compiler_params=params(12),
        cost_estimate=cost(1 << 28, 1 << 11, 1 << 18),
        name="count",
    )(wave_index)
    coeffs, table, kinds, lists, home = pl.pallas_call(
        weight_kernel,
        out_shape=(
            whole((128, 8, 128)),
            whole((16, 128)),
            whole((1, 256)),
            whole((4, 128), i32),
            whole((6,), i32),
        ),
        in_specs=[vmem, vmem],
        out_specs=(vmem, vmem, vmem, vmem, SMEM),
        scratch_shapes=[pltpu.VMEM((128, 16, 128), f32)],
        compiler_params=params(12),
        cost_estimate=cost(1 << 27, 1 << 11, 1 << 20),
        name="weight",
    )(sent, weights)
    coeffs = lax.all_to_all(coeffs, ("gx", "yz"), 0, 0, tiled=True)

    hidden, offsets = pl.pallas_call(
        radial_kernel,
        out_shape=(whole((64, 64, 256), bf16), whole((3, 64, 256))),
        scratch_shapes=[pltpu.VMEM((64, 256), f32), pltpu.VMEM((64, 256), f32)],
        compiler_params=params(20),
        cost_estimate=cost(1 << 32, 1 << 22, 4 << 20),
        name="radial",
    )(table, neighbours.T, neighbour_count.reshape(1, 256), radial_in, radial_mid)

    moved_up, hidden = lax.optimization_barrier((moved_up, hidden))
    nearby = [
        pl.BlockSpec((1, 512, 128), lambda i, home, at=at: (home[at], 0, 0)) for at in range(6)
    ]
    send_halo = pl.pallas_call(
        halo_kernel,
        out_shape=whole((32, 512), bf16),
        grid_spec=pltpu.PrefetchScalarGridSpec(
            num_scalar_prefetch=1,
            grid=(1,),
            in_specs=nearby[0:2] + [blocks_of((1, 32))],
            out_specs=blocks_of((32, 512)),
        ),
        compiler_params=params(61),
        cost_estimate=cost(1 << 24, 0, 1 << 18),
        name="halo",
    )(home, moved_up, moved_up, halo_list.reshape(1, 32))
    send_halo, late_hidden, late_up = lax.optimization_barrier((send_halo, hidden, moved_up))
    near = pl.pallas_call(
        near_kernel,
        out_shape=whole((512, 384), bf16),
        grid_spec=pltpu.PrefetchScalarGridSpec(
            num_scalar_prefetch=1,
            grid=(1,),
            in_specs=nearby + [blocks_of((4, 128))],
            out_specs=blocks_of((512, 384)),
        ),
        compiler_params=params(12),
        cost_estimate=cost(1 << 28, 0, 1 << 20),
        name="near",
    )(home, *[late_up] * 6, lists)
    radials = pl.pallas_call(
        spread_kernel,
        out_shape=whole((64, 512, 256), bf16),
        in_specs=[vmem, vmem],
        out_specs=vmem,
        scratch_shapes=[pltpu.VMEM((512, 64), bf16)],
        compiler_params=params(12),
        cost_estimate=cost(6 << 30, 0, 18 << 20),
        name="spread",
    )(late_hidden, radial_out)
    up = [(i, (i + 1) % 8) for i in range(8)]
    left = lax.ppermute(send_halo, "gx", up)
    right = lax.ppermute(send_halo, "gx", [(b, a) for a, b in up])

    part = pl.pallas_call(
        field_kernel,
        out_shape=whole((24, 256)),
        scratch_shapes=[pltpu.VMEM((384, 128 * SLABS), f32)],
        compiler_params=params(20),
        cost_estimate=cost(1 << 31, 0, 3 << 20),
        name="field",
    )(coeffs, basis_high, basis_low, waves, features, skip_weight, field_weight, read_rows, force_row)

    returned = pl.pallas_call(
        message_kernel,
        out_shape=whole((16, 24, 128)),
        in_specs=[SMEM] + [vmem] * 11,
        out_specs=vmem,
        scratch_shapes=[pltpu.VMEM((512, 384), bf16), pltpu.VMEM((512, 256), f32)],
        compiler_params=params(12),
        cost_estimate=cost(12 << 30, 0, 4 << 20),
        name="message",
    )(
        home,
        near,
        left,
        right,
        neighbours.T,
        offsets,
        radials,
        kinds,
        prod_weight,
        out_weight,
        read_rows,
        force_row,
    )
    returned = lax.all_to_all(returned, "yz", 0, 0, tiled=True)
    forces, energies = pl.pallas_call(
        final_kernel,
        out_shape=(whole((3, 256)), whole((1, 256))),
        in_specs=[SMEM, vmem, vmem, vmem],
        compiler_params=params(12),
        cost_estimate=cost(1 << 14, 1 << 12, 1 << 16),
        name="final",
    )(move_dest, returned, part, read_vector.reshape(1, 16))
    return forces, energies.reshape(256)


def solution(mesh):
    whole_spec = P(("gx", "yz"))
    in_specs = (
        (P(None, ("gx", "yz")), whole_spec, P(("gx", "yz"), None))
        + (whole_spec,) * 3
        + (P(("gx", "yz"), None), whole_spec)
        + (P(),) * 13
    )
    out_specs = (P(None, ("gx", "yz")), whole_spec)
    return jax.shard_map(
        on_device, mesh=mesh, in_specs=in_specs, out_specs=out_specs, check_vma=False
    )
```

```python
import math

import jax
import jax.numpy as jnp
from jax import lax
from jax.experimental import pallas as pl
from jax.experimental.pallas import tpu as pltpu
from jax.sharding import PartitionSpec as P

f32, bf16, i32 = jnp.float32, jnp.bfloat16, jnp.int32
highest = lax.Precision.HIGHEST
two_pi = 2.0 * math.pi
cutoff_radius = 3.5
ewald_width = 0.1
ewald_scale = 0.01

NX, NY, NZ = 16, 32, 2
SLABS = 2 * NZ + 2
RADIAL_GROUP, SLOT_GROUP = 16, 16


def row_of(chunk, component):
    return 128 * chunk + 32 * component


def dot(a, b, ca, cb, precision=None):
    return lax.dot_general(
        a, b, (((ca,), (cb,)), ((), ())), precision=precision, preferred_element_type=f32
    )


def halves(v):
    high = v.astype(bf16)
    return high, (v - high.astype(f32)).astype(bf16)


def dot_halves(a, b, ca, cb):
    return dot(a[0], b[0], ca, cb) + (dot(a[0], b[1], ca, cb) + dot(a[1], b[0], ca, cb))


def silu(v):
    half = 0.5 * v
    return half + half * jnp.tanh(half)


def iota(shape, dim):
    return lax.broadcasted_iota(i32, shape, dim)


def turns(t):
    angle = two_pi * (t - jnp.floor(t + 0.5))
    return jnp.cos(angle), jnp.sin(angle)


def params(mebibytes=58):
    return pltpu.CompilerParams(vmem_limit_bytes=mebibytes << 20)


def cost(flops, transcendentals, moved):
    return pl.CostEstimate(flops=flops, transcendentals=transcendentals, bytes_accessed=moved)


SMEM = pl.BlockSpec(memory_space=pltpu.SMEM)


def up_kernel(feat, up, charge_weight, out, charges):
    charges[...] = dot(charge_weight[...], feat[:, 0:128], 1, 1)
    for b in range(2):
        for c in range(4):
            rows = feat[b * 128 : (b + 1) * 128, c * 128 : (c + 1) * 128]
            mapped = dot(up[min(c, 1)], rows, 0, 1).astype(bf16)
            for q in range(4):
                out[b, row_of(q, c) : row_of(q, c) + 32, :] = mapped[32 * q : 32 * (q + 1)]


def moment_kernel(
    dest, slot, charges_in, pos, species, halo, out, basis_high, basis_low, waves, basis, stage
):
    gx = lax.axis_index("gx").astype(f32)
    charges = charges_in[...]
    lane = iota((1, 256), 1)
    second = lane >= 128
    xyz = pos[...].astype(f32)
    along_x = xyz[0:1] + gx
    along_y = xyz[1:2] + jnp.where(second, dest[1], dest[0]).astype(f32)
    along_z = xyz[2:3]
    cos_x, sin_x = turns((iota((NX, 256), 0) + 1).astype(f32) * along_x * (1.0 / 8.0))
    cos_y, sin_y = turns((iota((NY, 256), 0) + 1).astype(f32) * along_y * (1.0 / 16.0))
    cos_z, sin_z = turns(iota((8, 256), 0).astype(f32) * along_z)
    pairs = [
        (cos_z[abs(z) : abs(z) + 1], sin_z[abs(z) : abs(z) + 1] * (1.0 if z >= 0 else -1.0))
        for z in range(-NZ, NZ + 1)
    ]
    for i, (c, s) in enumerate(pairs):
        at = i * 128
        basis[at : at + 32, 0:256] = cos_y * c
        basis[at + 32 : at + 64, 0:256] = sin_y * c
        basis[at + 64 : at + 96, 0:256] = cos_y * s
        basis[at + 96 : at + 128, 0:256] = sin_y * s
        basis[at : at + 32, 256:512] = -(cos_y * s)
        basis[at + 32 : at + 64, 256:512] = -(sin_y * s)
        basis[at + 64 : at + 96, 256:512] = cos_y * c
        basis[at + 96 : at + 128, 256:512] = sin_y * c
    at = 128 * (SLABS - 1)
    basis[at : at + 128, :] = jnp.zeros((128, 512), f32)
    for i, (c, s) in enumerate(pairs):
        basis[at + i : at + i + 1, 0:256] = c
        basis[at + i : at + i + 1, 256:512] = -s
        basis[at + 64 + i : at + 65 + i, 0:256] = s
        basis[at + 64 + i : at + 65 + i, 256:512] = c
    waves[0:8] = charges
    waves[8:24] = cos_x
    waves[24:40] = sin_x
    left_cos = (cos_x[:, None, :] * charges[None]).reshape(128, 256)
    left_sin = (sin_x[:, None, :] * charges[None]).reshape(128, 256)
    basis_high[...], basis_low[...] = halves(basis[...])
    left = halves(jnp.concatenate([left_cos, left_sin], axis=1))
    moments = dot_halves(left, (basis_high[...], basis_low[...]), 1, 1)
    for i in range(SLABS):
        stage[:, i, :] = moments[:, i * 128 : (i + 1) * 128]
    kinds = species[...].astype(f32)
    for b in range(2):
        cut = slice(b * 128, (b + 1) * 128)
        for m in range(3):
            stage[:, 6 + 3 * b + m, :] = jnp.broadcast_to(xyz[m : m + 1, cut], (128, 128))
        stage[:, 12 + b, :] = jnp.broadcast_to(kinds[:, cut], (128, 128))
    listed = jnp.concatenate([halo[...], jnp.zeros((1, 96), i32)], axis=1)
    at = iota((1, 128), 1)
    for b in range(2):
        listed = jnp.where(at == 32 + b, dest[b], listed)
        listed = jnp.where(at == 34 + b, slot[b], listed)
    stage[:, 14, :] = jnp.broadcast_to(listed.astype(f32), (128, 128))
    stage[:, 15, :] = jnp.zeros((128, 128), f32)
    out[...] = stage[...].astype(bf16)


def count_kernel(wave_index, out):
    own_x = (lax.axis_index("gx") * 16 + lax.axis_index("yz")) // 8 + 1
    kx, ky, kz = wave_index[0:1, :], wave_index[1:2, :], wave_index[2:3, :]
    count = kx.shape[1]
    ours = kx == own_x
    rank = iota((8, count), 0)
    z_rows = jnp.where(ours & (kz == rank - NZ), 1.0, 0.0).astype(bf16)
    flat_rows = jnp.where(ours & (ky == 0) & (rank == SLABS - 1), 1.0, 0.0).astype(bf16)
    z_any = jnp.where(kz == rank - NZ, 1.0, 0.0).astype(bf16)
    y_match = jnp.where(jnp.abs(ky) == iota((NY, count), 0) + 1, 1.0, 0.0)
    y_sign = jnp.where(ky < 0, -y_match, y_match)
    even = dot(z_rows, y_match.astype(bf16), 1, 1)
    odd = dot(z_rows, y_sign.astype(bf16), 1, 1)
    flat = dot(flat_rows, z_any, 1, 1)
    gap = jnp.zeros((8, 56), f32)
    even = jnp.concatenate([even] * 4, axis=1)
    odd = jnp.concatenate([odd] * 4, axis=1)
    flat = jnp.concatenate([flat, gap] * 2, axis=1)
    row, lane = iota((8, 128), 0), iota((8, 128), 1)
    in_flat = row == SLABS - 1
    x_wave = own_x.astype(f32) * (two_pi / 8.0)
    y_wave = jnp.where(in_flat, 0, lane % 32 + 1).astype(f32) * (two_pi / 16.0)
    z_wave = (jnp.where(in_flat, lane % 64, row) - NZ).astype(f32) * two_pi
    squared = x_wave * x_wave + y_wave * y_wave + z_wave * z_wave
    prefactor = 8.0 * math.pi * ewald_scale / 128.0
    weight = prefactor * jnp.exp(-0.5 * ewald_width * ewald_width * squared) / squared
    out[0:8] = weight * jnp.where(in_flat, flat, even)
    out[8:16] = weight * jnp.where(in_flat, 0.0, odd)


def weight_kernel(
    sent, weights, out, table_out, kinds_out, lists_out, home_out, stage
):
    stage[...] = sent[...].astype(f32)
    total = jnp.sum(stage[:, 0:8, :], axis=0)
    row, lane = iota((8, 128), 0), iota((8, 128), 1)
    total = jnp.where(row < SLABS, total, 0.0)
    far = pltpu.roll(total, 64, 1)
    group = lane // 32
    swapped = jnp.where(group % 2 == 0, pltpu.roll(far, 96, 1), pltpu.roll(far, 32, 1))
    swapped = jnp.where((group == 0) | (group == 3), -swapped, swapped)
    coefficient = total * weights[0:8] + swapped * weights[8:16]
    out[...] = jnp.broadcast_to(coefficient[None], out.shape)
    gx, yz = lax.axis_index("gx"), lax.axis_index("yz")
    targets = [
        (gx, yz),
        ((gx + 7) % 8, yz),
        ((gx + 1) % 8, yz),
        (gx, (yz + 15) % 16),
        (gx, (yz + 1) % 16),
    ]
    plan = jnp.transpose(stage[:, 14, :])
    row = iota((16, 128), 0)
    device = iota((16, 128), 1)
    want_x, want_y = jnp.full((16, 128), -1, i32), jnp.full((16, 128), -1, i32)
    for t, (tx, ty) in enumerate(targets):
        want_x = jnp.where(row // 2 == t, tx, want_x)
        want_y = jnp.where(row // 2 == t, ty, want_y)
    here = (device // 16 == want_x).astype(f32)
    want_y, want_slot = want_y.astype(f32), (row % 2).astype(f32)
    picks = []
    for b in range(2):
        match = (plan[32 + b : 33 + b] == want_y) & (plan[34 + b : 35 + b] == want_slot)
        picks.append(jnp.where(match, here, 0.0))
    exact = [pick.astype(bf16) for pick in picks]

    def from_home(first, step):
        return sum(
            dot(exact[b], stage[:, first + b * step, :].astype(bf16), 1, 0) for b in range(2)
        )

    xyz = [from_home(6 + m, 3) for m in range(3)]
    kinds = from_home(12, 1)
    kinds_out[...] = jnp.concatenate([kinds[0:1], kinds[1:2]], axis=1)
    both = picks[0] + picks[1]
    column = 2.0 * both * (device % 16).astype(f32) + picks[1]
    for i, r in enumerate((0, 1, 6, 7, 8, 9)):
        home_out[i] = jnp.sum(jnp.where(row == r, column, 0.0)).astype(i32)
    lane = iota((1, 128), 1)
    atom = iota((128, 128), 0)
    ghosts = jnp.zeros((8, 128), f32)
    for t, (tx, ty) in enumerate(targets[1:]):
        listed = stage[tx * 16 + ty, 14:15, :].astype(i32)
        if t:
            listed = pltpu.roll(listed, 32 * t, 1)
        listed = jnp.where(lane // 32 == t, listed, -1)
        lists_out[t : t + 1] = listed
        for s in range(2):
            at = 2 * (t + 1) + s
            rows = jnp.concatenate(
                [x[at : at + 1] for x in xyz] + [jnp.zeros((5, 128), f32)], axis=0
            )
            chosen = jnp.where(atom + 128 * s == listed, 1.0, 0.0).astype(bf16)
            ghosts = ghosts + dot(rows.astype(bf16), chosen, 1, 0)
    part = lane // 32
    shifts = [
        jnp.where(part == 0, -1.0, jnp.where(part == 1, 1.0, 0.0)),
        jnp.where(part == 2, -1.0, jnp.where(part == 3, 1.0, 0.0)),
        jnp.zeros((1, 128), f32),
    ]
    zero = jnp.zeros((1, 128), f32)
    rows = [v for m in range(3) for v in (xyz[m][0:1], xyz[m][1:2], ghosts[m : m + 1] + shifts[m])]
    table_out[...] = jnp.concatenate(rows + [zero] * 7, axis=0)


def field_kernel(
    coeffs,
    basis_high,
    basis_low,
    waves,
    feat,
    skip_weight,
    field_weight,
    read_weight,
    force_weight,
    out,
    stacked,
):
    lane = iota((128, 128), 1)
    group_even = (lane // 32) % 2 == 0
    low_half = lane < 64
    y_wave = (lane % 32 + 1).astype(f32) * (two_pi / 16.0)
    for i in range(SLABS):
        cut = slice(i * 128, (i + 1) * 128)
        c = coeffs[:, i, :]
        stacked[0:128, cut] = c
        half = pltpu.roll(c, 64, 1)
        if i < SLABS - 1:
            moved = jnp.where(group_even, pltpu.roll(c, 96, 1), -pltpu.roll(c, 32, 1))
            stacked[128:256, cut] = y_wave * moved
            z_wave = two_pi * (i - NZ)
        else:
            stacked[128:256, cut] = jnp.zeros((128, 128), f32)
            z_wave = (lane % 64 - NZ).astype(f32) * two_pi
        stacked[256:384, cut] = z_wave * jnp.where(low_half, half, -half)
    grid = dot_halves(halves(stacked[...]), (basis_high[...], basis_low[...]), 1, 0)
    charges = waves[0:8]
    cos_x = jnp.broadcast_to(waves[8:24][:, None, :], (NX, 8, 256)).reshape(128, 256)
    sin_x = jnp.broadcast_to(waves[24:40][:, None, :], (NX, 8, 256)).reshape(128, 256)
    x_wave = (iota((128, 256), 0) // 8 + 1).astype(f32) * (two_pi / 8.0)

    def channels(v):
        return jnp.sum(v.reshape(NX, 8, 256), axis=0)

    def even_part(at):
        return channels(cos_x * grid[at : at + 128, 0:256] + sin_x * grid[at : at + 128, 256:512])

    potential = even_part(0)
    field = [
        channels(x_wave * (sin_x * grid[0:128, 0:256] - cos_x * grid[0:128, 256:512])),
        -even_part(128),
        -even_part(256),
    ]
    scalars = dot(field_weight[...], potential, 0, 0, highest) + dot(
        skip_weight[0], feat[:, 0:128], 0, 1
    )
    out[0:16] = dot(read_weight[...].astype(f32), scalars, 1, 0, highest)
    for m in range(3):
        vector = dot(skip_weight[1], feat[:, (m + 1) * 128 : (m + 2) * 128], 0, 1)
        out[16 + m : 17 + m] = dot(force_weight[...], vector, 1, 0, highest) + jnp.sum(
            charges * field[m], axis=0, keepdims=True
        )
    out[19:20] = 0.5 * jnp.sum(charges * potential, axis=0, keepdims=True)
    out[20:24] = jnp.zeros((4, 256), f32)


def radial_kernel(
    table,
    neighbours,
    live,
    radial_in,
    radial_mid,
    hidden_out,
    offset_out,
    dist_stage,
    scale_stage,
):
    tables = [
        [jnp.broadcast_to(table[3 * m + i : 3 * m + i + 1], (8, 128)) for i in range(3)]
        for m in range(3)
    ]
    for n in range(0, 64, 8):
        for half in range(2):
            cut = slice(half * 128, (half + 1) * 128)
            index = neighbours[n : n + 8, cut]
            within, block = index & 127, index >> 7
            squared = jnp.zeros((8, 128), f32)
            for m in range(3):
                found = [
                    jnp.take_along_axis(table, within, axis=1, mode="promise_in_bounds")
                    for table in tables[m]
                ]
                picked = jnp.where(block == 0, found[0], jnp.where(block == 1, found[1], found[2]))
                offset = picked - tables[m][half]
                offset_out[m, n : n + 8, cut] = offset
                squared = squared + offset * offset
            dist = jnp.sqrt(squared)
            dist_stage[n : n + 8, cut] = dist
            u = dist * (1.0 / cutoff_radius)
            u6 = (u * u) * (u * u) * (u * u)
            envelope = 1.0 + u6 * (-28.0 + u * (48.0 - 21.0 * u))
            alive = iota((8, 128), 0) + n < live[:, cut]
            scale_stage[n : n + 8, cut] = jnp.where(alive, 0.125 * envelope, 0.0)
    first = jnp.transpose(radial_in[...].astype(f32)).astype(bf16)
    mid = [jnp.transpose(radial_mid[i].astype(f32)).astype(bf16) for i in range(2)]
    centre = iota((8, 256), 0).astype(f32) * (cutoff_radius / 7.0)

    def body(group, carry):
        start = group * RADIAL_GROUP
        rows = []
        for j in range(RADIAL_GROUP):
            away = dist_stage[pl.ds(start + j, 1), :] - centre
            rows.append(jnp.exp(-4.0 * (away * away)))
        hidden = silu(dot(first, jnp.concatenate(rows, axis=1).astype(bf16), 1, 0)).astype(bf16)
        hidden = silu(dot(mid[0], hidden, 1, 0)).astype(bf16)
        hidden = silu(dot(mid[1], hidden, 1, 0))
        for j in range(RADIAL_GROUP):
            scaled = hidden[:, j * 256 : (j + 1) * 256] * scale_stage[pl.ds(start + j, 1), :]
            hidden_out[start + j] = scaled.astype(bf16)
        return carry

    lax.fori_loop(0, 64 // RADIAL_GROUP, body, 0)


def spread_kernel(hidden, radial_out, out, spread):
    mapped = jnp.transpose(radial_out[...].astype(f32)).astype(bf16)
    for q in range(4):
        for c in range(4):
            at = 128 * c + 32 * q
            spread[row_of(q, c) : row_of(q, c) + 32] = mapped[at : at + 32]

    def body(group, carry):
        for j in range(SLOT_GROUP):
            n = group * SLOT_GROUP + j
            out[n] = dot(spread[...], hidden[n], 1, 0).astype(bf16)
        return carry

    lax.fori_loop(0, 64 // SLOT_GROUP, body, 0)


def near_kernel(home, own0, own1, low0, low1, high0, high1, lists, table):
    table[:, 0:128] = own0[0]
    table[:, 128:256] = own1[0]
    atom = iota((128, 128), 0)
    ghosts = jnp.zeros((512, 128), f32)
    for t, pair in ((2, (low0, low1)), (3, (high0, high1))):
        for s, block in enumerate(pair):
            chosen = jnp.where(atom + 128 * s == lists[t : t + 1], 1.0, 0.0).astype(bf16)
            ghosts = ghosts + dot(block[0], chosen, 1, 0)
    table[:, 256:384] = ghosts.astype(bf16)


def halo_kernel(home, first, second, halo, out):
    atom = iota((128, 32), 0)
    chosen = [jnp.where(atom + 128 * s == halo[...], 1.0, 0.0).astype(bf16) for s in range(2)]
    out[...] = (dot(chosen[0], first[0], 0, 1) + dot(chosen[1], second[0], 0, 1)).astype(bf16)


def message_kernel(
    home,
    near,
    left,
    right,
    neighbours,
    offsets,
    radials,
    kinds,
    prod_weight,
    out_weight,
    read_weight,
    force_weight,
    out,
    table,
    total,
):
    table[...] = near[...]
    odd = lax.axis_index("gx") % 2 == 1
    pair = [jnp.transpose(ghost[...].astype(f32)) for ghost in (left, right)]
    table[:, 256:288] = jnp.where(odd, pair[1], pair[0]).astype(bf16)
    table[:, 288:320] = jnp.where(odd, pair[0], pair[1]).astype(bf16)
    total[...] = jnp.zeros((512, 256), f32)
    own_place = iota((256, 256), 0).astype(f32).astype(bf16)
    ghost_place = iota((128, 256), 0).astype(f32).astype(bf16)

    def choice(n):
        row = neighbours[pl.ds(n, 1), :]
        own = jnp.where(row < 256, row, -1).astype(f32).astype(bf16)
        ghost = (row - 256).astype(f32).astype(bf16)
        one, none = jnp.ones((), bf16), jnp.zeros((), bf16)
        return jnp.concatenate(
            [jnp.where(own_place == own, one, none), jnp.where(ghost_place == ghost, one, none)],
            axis=0,
        )

    def body(group, carry):
        slots = [group * SLOT_GROUP + j for j in range(SLOT_GROUP)]
        chosen = [choice(n) for n in slots]
        away = [[offsets[m, pl.ds(n, 1), :] for m in range(3)] for n in slots]
        for q in range(4):
            rows = slice(128 * q, 128 * (q + 1))
            cuts = [slice(row_of(q, c), row_of(q, c) + 32) for c in range(4)]
            sums = [total[cut] for cut in cuts]
            for j, r in enumerate(away):
                up = dot(table[rows], chosen[j], 1, 0)
                radial = radials[slots[j], rows].astype(f32)
                u = [up[32 * c : 32 * (c + 1)] for c in range(4)]
                path = [radial[32 * c : 32 * (c + 1)] for c in range(4)]
                along = u[1] * r[0] + u[2] * r[1] + u[3] * r[2]
                sums[0] = sums[0] + path[0] * u[0] + path[1] * along
                scalar = path[2] * u[0]
                for m in range(3):
                    sums[m + 1] = sums[m + 1] + scalar * r[m] + path[3] * u[m + 1]
            for cut, value in zip(cuts, sums):
                total[cut] = value
        return carry

    lax.fori_loop(0, 64 // SLOT_GROUP, body, 0)
    finish_messages(total, home, kinds, prod_weight, out_weight, read_weight, force_weight, out)


def finish_messages(
    total, home, kinds, prod_weight, out_weight, read_weight, force_weight, out
):
    kind = jnp.where(iota((6, 256), 0).astype(f32) == kinds[...], 1.0, 0.0)
    high, mid = halves(prod_weight[...])
    low = (prod_weight[...] - high.astype(f32) - mid.astype(f32)).astype(bf16)
    kind = kind.astype(bf16)
    paths = dot(high, kind, 0, 0) + (dot(mid, kind, 0, 0) + dot(low, kind, 0, 0))
    p = [paths[128 * i : 128 * (i + 1)] for i in range(5)]
    a0, *a1 = [
        jnp.concatenate([total[row_of(q, c) : row_of(q, c) + 32] for q in range(4)], axis=0)
        for c in range(4)
    ]
    square = a1[0] * a1[0] + a1[1] * a1[1] + a1[2] * a1[2]
    b0 = (p[0] * a0 + p[1] * a0 * a0 + p[2] * square).astype(bf16)
    rows = [dot(read_weight[...].astype(f32), dot(out_weight[0], b0, 0, 0), 1, 0, highest)]
    for m in range(3):
        b1 = (p[3] * a1[m] + p[4] * a0 * a1[m]).astype(bf16)
        rows.append(dot(force_weight[...], dot(out_weight[1], b1, 0, 0), 1, 0, highest))
    rows.append(jnp.zeros((5, 256), f32))
    result = jnp.concatenate(rows, axis=0)
    out[...] = jnp.zeros(out.shape, f32)
    for s in range(2):
        out[home[s] // 2] = result[:, s * 128 : (s + 1) * 128]


def final_kernel(dest, sent, own, read_vector, forces, energies):
    for b in range(2):
        cut = slice(b * 128, (b + 1) * 128)
        both = own[:, cut] + sent[dest[b]]
        forces[:, cut] = both[16:19]
        energies[:, cut] = (
            dot(read_vector[...], silu(both[0:16]), 1, 0, highest) + both[19:20]
        )


def whole(shape, dtype=f32):
    return jax.ShapeDtypeStruct(shape, dtype)


def blocks_of(shape):
    return pl.BlockSpec(shape, lambda i, home: (0,) * len(shape))


def on_device(
    positions,
    species,
    features,
    move_dest,
    move_slot,
    halo_list,
    neighbours,
    neighbour_count,
    wave_index,
    radial_in,
    radial_mid,
    radial_out,
    up_weight,
    prod_weight,
    out_weight,
    skip_weight,
    charge_weight,
    field_weight,
    read_weight,
    read_vector,
    force_weight,
):
    force_row = force_weight.reshape(1, 128)
    vmem = pl.BlockSpec(memory_space=pltpu.VMEM)

    read_rows = read_weight.T
    send_up, charges = pl.pallas_call(
        up_kernel,
        out_shape=(whole((2, 512, 128), bf16), whole((8, 256))),
        compiler_params=params(),
        cost_estimate=cost(1 << 25, 0, 1 << 20),
        name="up",
    )(features, up_weight, charge_weight.T)
    moved_up = lax.all_gather(send_up, "yz", axis=0, tiled=True)

    moments, basis_high, basis_low, waves = pl.pallas_call(
        moment_kernel,
        out_shape=(
            whole((128, 16, 128), bf16),
            whole((128 * SLABS, 512), bf16),
            whole((128 * SLABS, 512), bf16),
            whole((40, 256)),
        ),
        in_specs=[SMEM] * 2 + [vmem] * 4,
        scratch_shapes=[
            pltpu.VMEM((128 * SLABS, 512), f32),
            pltpu.VMEM((128, 16, 128), f32),
        ],
        compiler_params=params(20),
        cost_estimate=cost(1 << 30, 1 << 15, 3 << 20),
        name="moment",
    )(
        move_dest,
        move_slot,
        charges,
        positions,
        species.reshape(1, 256),
        halo_list.reshape(1, 32),
    )
    sent = lax.all_to_all(moments, ("gx", "yz"), 0, 0, tiled=True)
    weights = pl.pallas_call(
        count_kernel,
        out_shape=whole((16, 128)),
        compiler_params=params(12),
        cost_estimate=cost(1 << 28, 1 << 11, 1 << 18),
        name="count",
    )(wave_index)
    coeffs, table, kinds, lists, home = pl.pallas_call(
        weight_kernel,
        out_shape=(
            whole((128, 8, 128)),
            whole((16, 128)),
            whole((1, 256)),
            whole((4, 128), i32),
            whole((6,), i32),
        ),
        in_specs=[vmem, vmem],
        out_specs=(vmem, vmem, vmem, vmem, SMEM),
        scratch_shapes=[pltpu.VMEM((128, 16, 128), f32)],
        compiler_params=params(12),
        cost_estimate=cost(1 << 27, 1 << 11, 1 << 20),
        name="weight",
    )(sent, weights)
    coeffs = lax.all_to_all(coeffs, ("gx", "yz"), 0, 0, tiled=True)

    hidden, offsets = pl.pallas_call(
        radial_kernel,
        out_shape=(whole((64, 64, 256), bf16), whole((3, 64, 256))),
        scratch_shapes=[pltpu.VMEM((64, 256), f32), pltpu.VMEM((64, 256), f32)],
        compiler_params=params(20),
        cost_estimate=cost(1 << 32, 1 << 22, 4 << 20),
        name="radial",
    )(table, neighbours.T, neighbour_count.reshape(1, 256), radial_in, radial_mid)

    moved_up, hidden = lax.optimization_barrier((moved_up, hidden))
    nearby = [
        pl.BlockSpec((1, 512, 128), lambda i, home, at=at: (home[at], 0, 0)) for at in range(6)
    ]
    send_halo = pl.pallas_call(
        halo_kernel,
        out_shape=whole((32, 512), bf16),
        grid_spec=pltpu.PrefetchScalarGridSpec(
            num_scalar_prefetch=1,
            grid=(1,),
            in_specs=nearby[0:2] + [blocks_of((1, 32))],
            out_specs=blocks_of((32, 512)),
        ),
        compiler_params=params(61),
        cost_estimate=cost(1 << 24, 0, 1 << 18),
        name="halo",
    )(home, moved_up, moved_up, halo_list.reshape(1, 32))
    send_halo, late_hidden, late_up = lax.optimization_barrier((send_halo, hidden, moved_up))
    near = pl.pallas_call(
        near_kernel,
        out_shape=whole((512, 384), bf16),
        grid_spec=pltpu.PrefetchScalarGridSpec(
            num_scalar_prefetch=1,
            grid=(1,),
            in_specs=nearby + [blocks_of((4, 128))],
            out_specs=blocks_of((512, 384)),
        ),
        compiler_params=params(12),
        cost_estimate=cost(1 << 28, 0, 1 << 20),
        name="near",
    )(home, *[late_up] * 6, lists)
    radials = pl.pallas_call(
        spread_kernel,
        out_shape=whole((64, 512, 256), bf16),
        in_specs=[vmem, vmem],
        out_specs=vmem,
        scratch_shapes=[pltpu.VMEM((512, 64), bf16)],
        compiler_params=params(12),
        cost_estimate=cost(6 << 30, 0, 18 << 20),
        name="spread",
    )(late_hidden, radial_out)
    up = [(i, (i + 1) % 8) for i in range(8)]
    first = [pair for a, b in up[1::2] for pair in ((a, b), (b, a))]
    second = [pair for a, b in up[0::2] for pair in ((a, b), (b, a))]
    left = lax.ppermute(send_halo, "gx", first)
    right = lax.ppermute(send_halo, "gx", second)

    part = pl.pallas_call(
        field_kernel,
        out_shape=whole((24, 256)),
        scratch_shapes=[pltpu.VMEM((384, 128 * SLABS), f32)],
        compiler_params=params(20),
        cost_estimate=cost(1 << 31, 0, 3 << 20),
        name="field",
    )(coeffs, basis_high, basis_low, waves, features, skip_weight, field_weight, read_rows, force_row)

    returned = pl.pallas_call(
        message_kernel,
        out_shape=whole((16, 24, 128)),
        in_specs=[SMEM] + [vmem] * 11,
        out_specs=vmem,
        scratch_shapes=[pltpu.VMEM((512, 384), bf16), pltpu.VMEM((512, 256), f32)],
        compiler_params=params(12),
        cost_estimate=cost(12 << 30, 0, 4 << 20),
        name="message",
    )(
        home,
        near,
        left,
        right,
        neighbours.T,
        offsets,
        radials,
        kinds,
        prod_weight,
        out_weight,
        read_rows,
        force_row,
    )
    returned = lax.all_to_all(returned, "yz", 0, 0, tiled=True)
    forces, energies = pl.pallas_call(
        final_kernel,
        out_shape=(whole((3, 256)), whole((1, 256))),
        in_specs=[SMEM, vmem, vmem, vmem],
        compiler_params=params(12),
        cost_estimate=cost(1 << 14, 1 << 12, 1 << 16),
        name="final",
    )(move_dest, returned, part, read_vector.reshape(1, 16))
    return forces, energies.reshape(256)


def solution(mesh):
    whole_spec = P(("gx", "yz"))
    in_specs = (
        (P(None, ("gx", "yz")), whole_spec, P(("gx", "yz"), None))
        + (whole_spec,) * 3
        + (P(("gx", "yz"), None), whole_spec)
        + (P(),) * 13
    )
    out_specs = (P(None, ("gx", "yz")), whole_spec)
    return jax.shard_map(
        on_device, mesh=mesh, in_specs=in_specs, out_specs=out_specs, check_vma=False
    )
```

```python
import math

import jax
import jax.numpy as jnp
from jax import lax
from jax.experimental import pallas as pl
from jax.experimental.pallas import tpu as pltpu
from jax.sharding import PartitionSpec as P

f32, bf16, i32 = jnp.float32, jnp.bfloat16, jnp.int32
highest = lax.Precision.HIGHEST
two_pi = 2.0 * math.pi
cutoff_radius = 3.5
ewald_width = 0.1
ewald_scale = 0.01

NX, NY, NZ = 16, 32, 2
SLABS = 2 * NZ + 2
RADIAL_GROUP, SLOT_GROUP = 16, 16


def row_of(chunk, component):
    return 128 * chunk + 32 * component


def dot(a, b, ca, cb, precision=None):
    return lax.dot_general(
        a, b, (((ca,), (cb,)), ((), ())), precision=precision, preferred_element_type=f32
    )


def halves(v):
    high = v.astype(bf16)
    return high, (v - high.astype(f32)).astype(bf16)


def dot_halves(a, b, ca, cb):
    return dot(a[0], b[0], ca, cb) + (dot(a[0], b[1], ca, cb) + dot(a[1], b[0], ca, cb))


def silu(v):
    half = 0.5 * v
    return half + half * jnp.tanh(half)


def iota(shape, dim):
    return lax.broadcasted_iota(i32, shape, dim)


def turns(t):
    angle = two_pi * (t - jnp.floor(t + 0.5))
    return jnp.cos(angle), jnp.sin(angle)


def params(mebibytes=58):
    return pltpu.CompilerParams(vmem_limit_bytes=mebibytes << 20)


def cost(flops, transcendentals, moved):
    return pl.CostEstimate(flops=flops, transcendentals=transcendentals, bytes_accessed=moved)


SMEM = pl.BlockSpec(memory_space=pltpu.SMEM)


def up_kernel(feat, up, charge_weight, out, charges):
    charges[...] = dot(charge_weight[...], feat[:, 0:128], 1, 1)
    for b in range(2):
        for c in range(4):
            rows = feat[b * 128 : (b + 1) * 128, c * 128 : (c + 1) * 128]
            mapped = dot(up[min(c, 1)], rows, 0, 1).astype(bf16)
            for q in range(4):
                out[b, row_of(q, c) : row_of(q, c) + 32, :] = mapped[32 * q : 32 * (q + 1)]


def moment_kernel(
    dest, slot, charges_in, pos, species, halo, out, basis_high, basis_low, waves, basis, stage
):
    gx = lax.axis_index("gx").astype(f32)
    charges = charges_in[...]
    lane = iota((1, 256), 1)
    second = lane >= 128
    xyz = pos[...].astype(f32)
    along_x = xyz[0:1] + gx
    along_y = xyz[1:2] + jnp.where(second, dest[1], dest[0]).astype(f32)
    along_z = xyz[2:3]
    cos_x, sin_x = turns((iota((NX, 256), 0) + 1).astype(f32) * along_x * (1.0 / 8.0))
    cos_y, sin_y = turns((iota((NY, 256), 0) + 1).astype(f32) * along_y * (1.0 / 16.0))
    cos_z, sin_z = turns(iota((8, 256), 0).astype(f32) * along_z)
    pairs = [
        (cos_z[abs(z) : abs(z) + 1], sin_z[abs(z) : abs(z) + 1] * (1.0 if z >= 0 else -1.0))
        for z in range(-NZ, NZ + 1)
    ]
    for i, (c, s) in enumerate(pairs):
        at = i * 128
        basis[at : at + 32, 0:256] = cos_y * c
        basis[at + 32 : at + 64, 0:256] = sin_y * c
        basis[at + 64 : at + 96, 0:256] = cos_y * s
        basis[at + 96 : at + 128, 0:256] = sin_y * s
        basis[at : at + 32, 256:512] = -(cos_y * s)
        basis[at + 32 : at + 64, 256:512] = -(sin_y * s)
        basis[at + 64 : at + 96, 256:512] = cos_y * c
        basis[at + 96 : at + 128, 256:512] = sin_y * c
    at = 128 * (SLABS - 1)
    basis[at : at + 128, :] = jnp.zeros((128, 512), f32)
    for i, (c, s) in enumerate(pairs):
        basis[at + i : at + i + 1, 0:256] = c
        basis[at + i : at + i + 1, 256:512] = -s
        basis[at + 64 + i : at + 65 + i, 0:256] = s
        basis[at + 64 + i : at + 65 + i, 256:512] = c
    waves[0:8] = charges
    waves[8:24] = cos_x
    waves[24:40] = sin_x
    left_cos = (cos_x[:, None, :] * charges[None]).reshape(128, 256)
    left_sin = (sin_x[:, None, :] * charges[None]).reshape(128, 256)
    basis_high[...], basis_low[...] = halves(basis[...])
    left = halves(jnp.concatenate([left_cos, left_sin], axis=1))
    moments = dot_halves(left, (basis_high[...], basis_low[...]), 1, 1)
    for i in range(SLABS):
        stage[:, i, :] = moments[:, i * 128 : (i + 1) * 128]
    kinds = species[...].astype(f32)
    for b in range(2):
        cut = slice(b * 128, (b + 1) * 128)
        for m in range(3):
            stage[:, 6 + 3 * b + m, :] = jnp.broadcast_to(xyz[m : m + 1, cut], (128, 128))
        stage[:, 12 + b, :] = jnp.broadcast_to(kinds[:, cut], (128, 128))
    listed = jnp.concatenate([halo[...], jnp.zeros((1, 96), i32)], axis=1)
    at = iota((1, 128), 1)
    for b in range(2):
        listed = jnp.where(at == 32 + b, dest[b], listed)
        listed = jnp.where(at == 34 + b, slot[b], listed)
    stage[:, 14, :] = jnp.broadcast_to(listed.astype(f32), (128, 128))
    stage[:, 15, :] = jnp.zeros((128, 128), f32)
    out[...] = stage[...].astype(bf16)


def count_kernel(wave_index, out):
    own_x = (lax.axis_index("gx") * 16 + lax.axis_index("yz")) // 8 + 1
    kx, ky, kz = wave_index[0:1, :], wave_index[1:2, :], wave_index[2:3, :]
    count = kx.shape[1]
    ours = kx == own_x
    rank = iota((8, count), 0)
    z_rows = jnp.where(ours & (kz == rank - NZ), 1.0, 0.0).astype(bf16)
    flat_rows = jnp.where(ours & (ky == 0) & (rank == SLABS - 1), 1.0, 0.0).astype(bf16)
    z_any = jnp.where(kz == rank - NZ, 1.0, 0.0).astype(bf16)
    y_match = jnp.where(jnp.abs(ky) == iota((NY, count), 0) + 1, 1.0, 0.0)
    y_sign = jnp.where(ky < 0, -y_match, y_match)
    even = dot(z_rows, y_match.astype(bf16), 1, 1)
    odd = dot(z_rows, y_sign.astype(bf16), 1, 1)
    flat = dot(flat_rows, z_any, 1, 1)
    gap = jnp.zeros((8, 56), f32)
    even = jnp.concatenate([even] * 4, axis=1)
    odd = jnp.concatenate([odd] * 4, axis=1)
    flat = jnp.concatenate([flat, gap] * 2, axis=1)
    row, lane = iota((8, 128), 0), iota((8, 128), 1)
    in_flat = row == SLABS - 1
    x_wave = own_x.astype(f32) * (two_pi / 8.0)
    y_wave = jnp.where(in_flat, 0, lane % 32 + 1).astype(f32) * (two_pi / 16.0)
    z_wave = (jnp.where(in_flat, lane % 64, row) - NZ).astype(f32) * two_pi
    squared = x_wave * x_wave + y_wave * y_wave + z_wave * z_wave
    prefactor = 8.0 * math.pi * ewald_scale / 128.0
    weight = prefactor * jnp.exp(-0.5 * ewald_width * ewald_width * squared) / squared
    out[0:8] = weight * jnp.where(in_flat, flat, even)
    out[8:16] = weight * jnp.where(in_flat, 0.0, odd)


def weight_kernel(
    sent, weights, out, table_out, kinds_out, lists_out, home_out, stage
):
    stage[...] = sent[...].astype(f32)
    total = jnp.sum(stage[:, 0:8, :], axis=0)
    row, lane = iota((8, 128), 0), iota((8, 128), 1)
    total = jnp.where(row < SLABS, total, 0.0)
    far = pltpu.roll(total, 64, 1)
    group = lane // 32
    swapped = jnp.where(group % 2 == 0, pltpu.roll(far, 96, 1), pltpu.roll(far, 32, 1))
    swapped = jnp.where((group == 0) | (group == 3), -swapped, swapped)
    coefficient = total * weights[0:8] + swapped * weights[8:16]
    out[...] = jnp.broadcast_to(coefficient[None], out.shape)
    gx, yz = lax.axis_index("gx"), lax.axis_index("yz")
    targets = [
        (gx, yz),
        ((gx + 7) % 8, yz),
        ((gx + 1) % 8, yz),
        (gx, (yz + 15) % 16),
        (gx, (yz + 1) % 16),
    ]
    plan = jnp.transpose(stage[:, 14, :])
    row = iota((16, 128), 0)
    device = iota((16, 128), 1)
    want_x, want_y = jnp.full((16, 128), -1, i32), jnp.full((16, 128), -1, i32)
    for t, (tx, ty) in enumerate(targets):
        want_x = jnp.where(row // 2 == t, tx, want_x)
        want_y = jnp.where(row // 2 == t, ty, want_y)
    here = (device // 16 == want_x).astype(f32)
    want_y, want_slot = want_y.astype(f32), (row % 2).astype(f32)
    picks = []
    for b in range(2):
        match = (plan[32 + b : 33 + b] == want_y) & (plan[34 + b : 35 + b] == want_slot)
        picks.append(jnp.where(match, here, 0.0))
    exact = [pick.astype(bf16) for pick in picks]

    def from_home(first, step):
        return sum(
            dot(exact[b], stage[:, first + b * step, :].astype(bf16), 1, 0) for b in range(2)
        )

    xyz = [from_home(6 + m, 3) for m in range(3)]
    kinds = from_home(12, 1)
    kinds_out[...] = jnp.concatenate([kinds[0:1], kinds[1:2]], axis=1)
    both = picks[0] + picks[1]
    column = 2.0 * both * (device % 16).astype(f32) + picks[1]
    for i, r in enumerate((0, 1, 6, 7, 8, 9)):
        home_out[i] = jnp.sum(jnp.where(row == r, column, 0.0)).astype(i32)
    lane = iota((1, 128), 1)
    atom = iota((128, 128), 0)
    ghosts = jnp.zeros((8, 128), f32)
    for t, (tx, ty) in enumerate(targets[1:]):
        listed = stage[tx * 16 + ty, 14:15, :].astype(i32)
        if t:
            listed = pltpu.roll(listed, 32 * t, 1)
        listed = jnp.where(lane // 32 == t, listed, -1)
        lists_out[t : t + 1] = listed
        for s in range(2):
            at = 2 * (t + 1) + s
            rows = jnp.concatenate(
                [x[at : at + 1] for x in xyz] + [jnp.zeros((5, 128), f32)], axis=0
            )
            chosen = jnp.where(atom + 128 * s == listed, 1.0, 0.0).astype(bf16)
            ghosts = ghosts + dot(rows.astype(bf16), chosen, 1, 0)
    part = lane // 32
    shifts = [
        jnp.where(part == 0, -1.0, jnp.where(part == 1, 1.0, 0.0)),
        jnp.where(part == 2, -1.0, jnp.where(part == 3, 1.0, 0.0)),
        jnp.zeros((1, 128), f32),
    ]
    zero = jnp.zeros((1, 128), f32)
    rows = [v for m in range(3) for v in (xyz[m][0:1], xyz[m][1:2], ghosts[m : m + 1] + shifts[m])]
    table_out[...] = jnp.concatenate(rows + [zero] * 7, axis=0)


def field_kernel(
    coeffs,
    basis_high,
    basis_low,
    waves,
    feat,
    skip_weight,
    field_weight,
    read_weight,
    force_weight,
    out,
    stacked,
):
    lane = iota((128, 128), 1)
    group_even = (lane // 32) % 2 == 0
    low_half = lane < 64
    y_wave = (lane % 32 + 1).astype(f32) * (two_pi / 16.0)
    for i in range(SLABS):
        cut = slice(i * 128, (i + 1) * 128)
        c = coeffs[:, i, :]
        stacked[0:128, cut] = c
        half = pltpu.roll(c, 64, 1)
        if i < SLABS - 1:
            moved = jnp.where(group_even, pltpu.roll(c, 96, 1), -pltpu.roll(c, 32, 1))
            stacked[128:256, cut] = y_wave * moved
            z_wave = two_pi * (i - NZ)
        else:
            stacked[128:256, cut] = jnp.zeros((128, 128), f32)
            z_wave = (lane % 64 - NZ).astype(f32) * two_pi
        stacked[256:384, cut] = z_wave * jnp.where(low_half, half, -half)
    grid = dot_halves(halves(stacked[...]), (basis_high[...], basis_low[...]), 1, 0)
    charges = waves[0:8]
    cos_x = jnp.broadcast_to(waves[8:24][:, None, :], (NX, 8, 256)).reshape(128, 256)
    sin_x = jnp.broadcast_to(waves[24:40][:, None, :], (NX, 8, 256)).reshape(128, 256)
    x_wave = (iota((128, 256), 0) // 8 + 1).astype(f32) * (two_pi / 8.0)

    def channels(v):
        return jnp.sum(v.reshape(NX, 8, 256), axis=0)

    def even_part(at):
        return channels(cos_x * grid[at : at + 128, 0:256] + sin_x * grid[at : at + 128, 256:512])

    potential = even_part(0)
    field = [
        channels(x_wave * (sin_x * grid[0:128, 0:256] - cos_x * grid[0:128, 256:512])),
        -even_part(128),
        -even_part(256),
    ]
    scalars = dot(field_weight[...], potential, 0, 0, highest) + dot(
        skip_weight[0], feat[:, 0:128], 0, 1
    )
    out[0:16] = dot(read_weight[...].astype(f32), scalars, 1, 0, highest)
    for m in range(3):
        vector = dot(skip_weight[1], feat[:, (m + 1) * 128 : (m + 2) * 128], 0, 1)
        out[16 + m : 17 + m] = dot(force_weight[...], vector, 1, 0, highest) + jnp.sum(
            charges * field[m], axis=0, keepdims=True
        )
    out[19:20] = 0.5 * jnp.sum(charges * potential, axis=0, keepdims=True)
    out[20:24] = jnp.zeros((4, 256), f32)


def radial_kernel(
    table,
    neighbours,
    live,
    radial_in,
    radial_mid,
    hidden_out,
    offset_out,
    dist_stage,
    scale_stage,
):
    tables = [
        [jnp.broadcast_to(table[3 * m + i : 3 * m + i + 1], (8, 128)) for i in range(3)]
        for m in range(3)
    ]
    for n in range(0, 64, 8):
        for half in range(2):
            cut = slice(half * 128, (half + 1) * 128)
            index = neighbours[n : n + 8, cut]
            within, block = index & 127, index >> 7
            squared = jnp.zeros((8, 128), f32)
            for m in range(3):
                found = [
                    jnp.take_along_axis(table, within, axis=1, mode="promise_in_bounds")
                    for table in tables[m]
                ]
                picked = jnp.where(block == 0, found[0], jnp.where(block == 1, found[1], found[2]))
                offset = picked - tables[m][half]
                offset_out[m, n : n + 8, cut] = offset
                squared = squared + offset * offset
            dist = jnp.sqrt(squared)
            dist_stage[n : n + 8, cut] = dist
            u = dist * (1.0 / cutoff_radius)
            u6 = (u * u) * (u * u) * (u * u)
            envelope = 1.0 + u6 * (-28.0 + u * (48.0 - 21.0 * u))
            alive = iota((8, 128), 0) + n < live[:, cut]
            scale_stage[n : n + 8, cut] = jnp.where(alive, 0.125 * envelope, 0.0)
    first = jnp.transpose(radial_in[...].astype(f32)).astype(bf16)
    mid = [jnp.transpose(radial_mid[i].astype(f32)).astype(bf16) for i in range(2)]
    centre = iota((8, 256), 0).astype(f32) * (cutoff_radius / 7.0)

    def body(group, carry):
        start = group * RADIAL_GROUP
        rows = []
        for j in range(RADIAL_GROUP):
            away = dist_stage[pl.ds(start + j, 1), :] - centre
            rows.append(jnp.exp(-4.0 * (away * away)))
        hidden = silu(dot(first, jnp.concatenate(rows, axis=1).astype(bf16), 1, 0)).astype(bf16)
        hidden = silu(dot(mid[0], hidden, 1, 0)).astype(bf16)
        hidden = silu(dot(mid[1], hidden, 1, 0))
        for j in range(RADIAL_GROUP):
            scaled = hidden[:, j * 256 : (j + 1) * 256] * scale_stage[pl.ds(start + j, 1), :]
            hidden_out[start + j] = scaled.astype(bf16)
        return carry

    lax.fori_loop(0, 64 // RADIAL_GROUP, body, 0)


def spread_kernel(hidden, radial_out, out, spread):
    mapped = jnp.transpose(radial_out[...].astype(f32)).astype(bf16)
    for q in range(4):
        for c in range(4):
            at = 128 * c + 32 * q
            spread[row_of(q, c) : row_of(q, c) + 32] = mapped[at : at + 32]

    def body(group, carry):
        for j in range(SLOT_GROUP):
            n = group * SLOT_GROUP + j
            out[n] = dot(spread[...], hidden[n], 1, 0).astype(bf16)
        return carry

    lax.fori_loop(0, 64 // SLOT_GROUP, body, 0)


def near_kernel(home, own0, own1, low0, low1, high0, high1, lists, table):
    table[:, 0:128] = own0[0]
    table[:, 128:256] = own1[0]
    atom = iota((128, 128), 0)
    ghosts = jnp.zeros((512, 128), f32)
    for t, pair in ((2, (low0, low1)), (3, (high0, high1))):
        for s, block in enumerate(pair):
            chosen = jnp.where(atom + 128 * s == lists[t : t + 1], 1.0, 0.0).astype(bf16)
            ghosts = ghosts + dot(block[0], chosen, 1, 0)
    table[:, 256:384] = ghosts.astype(bf16)


def halo_kernel(home, first, second, halo, out):
    atom = iota((128, 32), 0)
    chosen = [jnp.where(atom + 128 * s == halo[...], 1.0, 0.0).astype(bf16) for s in range(2)]
    out[...] = (dot(chosen[0], first[0], 0, 1) + dot(chosen[1], second[0], 0, 1)).astype(bf16)


def message_kernel(
    home,
    near,
    left,
    right,
    neighbours,
    offsets,
    radials,
    kinds,
    prod_weight,
    out_weight,
    read_weight,
    force_weight,
    out,
    table,
    total,
):
    table[...] = near[...]
    even = lax.axis_index("gx") % 2 == 0
    pair = [jnp.transpose(ghost[...].astype(f32)) for ghost in (left, right)]
    table[:, 256:288] = jnp.where(even, pair[1], pair[0]).astype(bf16)
    table[:, 288:320] = jnp.where(even, pair[0], pair[1]).astype(bf16)
    total[...] = jnp.zeros((512, 256), f32)
    own_place = iota((256, 256), 0).astype(f32).astype(bf16)
    ghost_place = iota((128, 256), 0).astype(f32).astype(bf16)

    def choice(n):
        row = neighbours[pl.ds(n, 1), :]
        own = jnp.where(row < 256, row, -1).astype(f32).astype(bf16)
        ghost = (row - 256).astype(f32).astype(bf16)
        one, none = jnp.ones((), bf16), jnp.zeros((), bf16)
        return jnp.concatenate(
            [jnp.where(own_place == own, one, none), jnp.where(ghost_place == ghost, one, none)],
            axis=0,
        )

    def body(group, carry):
        slots = [group * SLOT_GROUP + j for j in range(SLOT_GROUP)]
        chosen = [choice(n) for n in slots]
        away = [[offsets[m, pl.ds(n, 1), :] for m in range(3)] for n in slots]
        for q in range(4):
            rows = slice(128 * q, 128 * (q + 1))
            cuts = [slice(row_of(q, c), row_of(q, c) + 32) for c in range(4)]
            sums = [total[cut] for cut in cuts]
            for j, r in enumerate(away):
                up = dot(table[rows], chosen[j], 1, 0)
                radial = radials[slots[j], rows].astype(f32)
                u = [up[32 * c : 32 * (c + 1)] for c in range(4)]
                path = [radial[32 * c : 32 * (c + 1)] for c in range(4)]
                along = u[1] * r[0] + u[2] * r[1] + u[3] * r[2]
                sums[0] = sums[0] + path[0] * u[0] + path[1] * along
                scalar = path[2] * u[0]
                for m in range(3):
                    sums[m + 1] = sums[m + 1] + scalar * r[m] + path[3] * u[m + 1]
            for cut, value in zip(cuts, sums):
                total[cut] = value
        return carry

    lax.fori_loop(0, 64 // SLOT_GROUP, body, 0)
    finish_messages(total, home, kinds, prod_weight, out_weight, read_weight, force_weight, out)


def finish_messages(
    total, home, kinds, prod_weight, out_weight, read_weight, force_weight, out
):
    kind = jnp.where(iota((6, 256), 0).astype(f32) == kinds[...], 1.0, 0.0)
    high, mid = halves(prod_weight[...])
    low = (prod_weight[...] - high.astype(f32) - mid.astype(f32)).astype(bf16)
    kind = kind.astype(bf16)
    paths = dot(high, kind, 0, 0) + (dot(mid, kind, 0, 0) + dot(low, kind, 0, 0))
    p = [paths[128 * i : 128 * (i + 1)] for i in range(5)]
    a0, *a1 = [
        jnp.concatenate([total[row_of(q, c) : row_of(q, c) + 32] for q in range(4)], axis=0)
        for c in range(4)
    ]
    square = a1[0] * a1[0] + a1[1] * a1[1] + a1[2] * a1[2]
    b0 = (p[0] * a0 + p[1] * a0 * a0 + p[2] * square).astype(bf16)
    rows = [dot(read_weight[...].astype(f32), dot(out_weight[0], b0, 0, 0), 1, 0, highest)]
    for m in range(3):
        b1 = (p[3] * a1[m] + p[4] * a0 * a1[m]).astype(bf16)
        rows.append(dot(force_weight[...], dot(out_weight[1], b1, 0, 0), 1, 0, highest))
    rows.append(jnp.zeros((5, 256), f32))
    result = jnp.concatenate(rows, axis=0)
    out[...] = jnp.zeros(out.shape, f32)
    for s in range(2):
        out[home[s] // 2] = result[:, s * 128 : (s + 1) * 128]


def final_kernel(dest, sent, own, read_vector, forces, energies):
    for b in range(2):
        cut = slice(b * 128, (b + 1) * 128)
        both = own[:, cut] + sent[dest[b]]
        forces[:, cut] = both[16:19]
        energies[:, cut] = (
            dot(read_vector[...], silu(both[0:16]), 1, 0, highest) + both[19:20]
        )


def whole(shape, dtype=f32):
    return jax.ShapeDtypeStruct(shape, dtype)


def blocks_of(shape):
    return pl.BlockSpec(shape, lambda i, home: (0,) * len(shape))


def on_device(
    positions,
    species,
    features,
    move_dest,
    move_slot,
    halo_list,
    neighbours,
    neighbour_count,
    wave_index,
    radial_in,
    radial_mid,
    radial_out,
    up_weight,
    prod_weight,
    out_weight,
    skip_weight,
    charge_weight,
    field_weight,
    read_weight,
    read_vector,
    force_weight,
):
    force_row = force_weight.reshape(1, 128)
    vmem = pl.BlockSpec(memory_space=pltpu.VMEM)

    read_rows = read_weight.T
    send_up, charges = pl.pallas_call(
        up_kernel,
        out_shape=(whole((2, 512, 128), bf16), whole((8, 256))),
        compiler_params=params(),
        cost_estimate=cost(1 << 25, 0, 1 << 20),
        name="up",
    )(features, up_weight, charge_weight.T)
    moved_up = lax.all_gather(send_up, "yz", axis=0, tiled=True)

    moments, basis_high, basis_low, waves = pl.pallas_call(
        moment_kernel,
        out_shape=(
            whole((128, 16, 128), bf16),
            whole((128 * SLABS, 512), bf16),
            whole((128 * SLABS, 512), bf16),
            whole((40, 256)),
        ),
        in_specs=[SMEM] * 2 + [vmem] * 4,
        scratch_shapes=[
            pltpu.VMEM((128 * SLABS, 512), f32),
            pltpu.VMEM((128, 16, 128), f32),
        ],
        compiler_params=params(20),
        cost_estimate=cost(1 << 30, 1 << 15, 3 << 20),
        name="moment",
    )(
        move_dest,
        move_slot,
        charges,
        positions,
        species.reshape(1, 256),
        halo_list.reshape(1, 32),
    )
    sent = lax.all_to_all(moments, ("gx", "yz"), 0, 0, tiled=True)
    weights = pl.pallas_call(
        count_kernel,
        out_shape=whole((16, 128)),
        compiler_params=params(12),
        cost_estimate=cost(1 << 28, 1 << 11, 1 << 18),
        name="count",
    )(wave_index)
    coeffs, table, kinds, lists, home = pl.pallas_call(
        weight_kernel,
        out_shape=(
            whole((128, 8, 128)),
            whole((16, 128)),
            whole((1, 256)),
            whole((4, 128), i32),
            whole((6,), i32),
        ),
        in_specs=[vmem, vmem],
        out_specs=(vmem, vmem, vmem, vmem, SMEM),
        scratch_shapes=[pltpu.VMEM((128, 16, 128), f32)],
        compiler_params=params(12),
        cost_estimate=cost(1 << 27, 1 << 11, 1 << 20),
        name="weight",
    )(sent, weights)
    coeffs = lax.all_to_all(coeffs, ("gx", "yz"), 0, 0, tiled=True)

    hidden, offsets = pl.pallas_call(
        radial_kernel,
        out_shape=(whole((64, 64, 256), bf16), whole((3, 64, 256))),
        scratch_shapes=[pltpu.VMEM((64, 256), f32), pltpu.VMEM((64, 256), f32)],
        compiler_params=params(20),
        cost_estimate=cost(1 << 32, 1 << 22, 4 << 20),
        name="radial",
    )(table, neighbours.T, neighbour_count.reshape(1, 256), radial_in, radial_mid)

    moved_up, hidden = lax.optimization_barrier((moved_up, hidden))
    nearby = [
        pl.BlockSpec((1, 512, 128), lambda i, home, at=at: (home[at], 0, 0)) for at in range(6)
    ]
    send_halo = pl.pallas_call(
        halo_kernel,
        out_shape=whole((32, 512), bf16),
        grid_spec=pltpu.PrefetchScalarGridSpec(
            num_scalar_prefetch=1,
            grid=(1,),
            in_specs=nearby[0:2] + [blocks_of((1, 32))],
            out_specs=blocks_of((32, 512)),
        ),
        compiler_params=params(61),
        cost_estimate=cost(1 << 24, 0, 1 << 18),
        name="halo",
    )(home, moved_up, moved_up, halo_list.reshape(1, 32))
    send_halo, late_hidden, late_up = lax.optimization_barrier((send_halo, hidden, moved_up))
    near = pl.pallas_call(
        near_kernel,
        out_shape=whole((512, 384), bf16),
        grid_spec=pltpu.PrefetchScalarGridSpec(
            num_scalar_prefetch=1,
            grid=(1,),
            in_specs=nearby + [blocks_of((4, 128))],
            out_specs=blocks_of((512, 384)),
        ),
        compiler_params=params(12),
        cost_estimate=cost(1 << 28, 0, 1 << 20),
        name="near",
    )(home, *[late_up] * 6, lists)
    radials = pl.pallas_call(
        spread_kernel,
        out_shape=whole((64, 512, 256), bf16),
        in_specs=[vmem, vmem],
        out_specs=vmem,
        scratch_shapes=[pltpu.VMEM((512, 64), bf16)],
        compiler_params=params(12),
        cost_estimate=cost(6 << 30, 0, 18 << 20),
        name="spread",
    )(late_hidden, radial_out)
    up = [(i, (i + 1) % 8) for i in range(8)]
    first = [pair for a, b in up[1::2] for pair in ((a, b), (b, a))]
    second = [pair for a, b in up[0::2] for pair in ((a, b), (b, a))]
    left = lax.ppermute(send_halo, "gx", second)
    right = lax.ppermute(send_halo, "gx", first)

    part = pl.pallas_call(
        field_kernel,
        out_shape=whole((24, 256)),
        scratch_shapes=[pltpu.VMEM((384, 128 * SLABS), f32)],
        compiler_params=params(20),
        cost_estimate=cost(1 << 31, 0, 3 << 20),
        name="field",
    )(coeffs, basis_high, basis_low, waves, features, skip_weight, field_weight, read_rows, force_row)

    returned = pl.pallas_call(
        message_kernel,
        out_shape=whole((16, 24, 128)),
        in_specs=[SMEM] + [vmem] * 11,
        out_specs=vmem,
        scratch_shapes=[pltpu.VMEM((512, 384), bf16), pltpu.VMEM((512, 256), f32)],
        compiler_params=params(12),
        cost_estimate=cost(12 << 30, 0, 4 << 20),
        name="message",
    )(
        home,
        near,
        left,
        right,
        neighbours.T,
        offsets,
        radials,
        kinds,
        prod_weight,
        out_weight,
        read_rows,
        force_row,
    )
    returned = lax.all_to_all(returned, "yz", 0, 0, tiled=True)
    forces, energies = pl.pallas_call(
        final_kernel,
        out_shape=(whole((3, 256)), whole((1, 256))),
        in_specs=[SMEM, vmem, vmem, vmem],
        compiler_params=params(12),
        cost_estimate=cost(1 << 14, 1 << 12, 1 << 16),
        name="final",
    )(move_dest, returned, part, read_vector.reshape(1, 16))
    return forces, energies.reshape(256)


def solution(mesh):
    whole_spec = P(("gx", "yz"))
    in_specs = (
        (P(None, ("gx", "yz")), whole_spec, P(("gx", "yz"), None))
        + (whole_spec,) * 3
        + (P(("gx", "yz"), None), whole_spec)
        + (P(),) * 13
    )
    out_specs = (P(None, ("gx", "yz")), whole_spec)
    return jax.shard_map(
        on_device, mesh=mesh, in_specs=in_specs, out_specs=out_specs, check_vma=False
    )
```

```python
import math

import jax
import jax.numpy as jnp
from jax import lax
from jax.experimental import pallas as pl
from jax.experimental.pallas import tpu as pltpu
from jax.sharding import PartitionSpec as P

f32, bf16, i32 = jnp.float32, jnp.bfloat16, jnp.int32
highest = lax.Precision.HIGHEST
two_pi = 2.0 * math.pi
cutoff_radius = 3.5
ewald_width = 0.1
ewald_scale = 0.01

NX, NY, NZ = 16, 32, 2
SLABS = 2 * NZ + 2
RADIAL_GROUP, SLOT_GROUP = 32, 16


def row_of(chunk, component):
    return 128 * chunk + 32 * component


def dot(a, b, ca, cb, precision=None):
    return lax.dot_general(
        a, b, (((ca,), (cb,)), ((), ())), precision=precision, preferred_element_type=f32
    )


def halves(v):
    high = v.astype(bf16)
    return high, (v - high.astype(f32)).astype(bf16)


def dot_halves(a, b, ca, cb):
    return dot(a[0], b[0], ca, cb) + (dot(a[0], b[1], ca, cb) + dot(a[1], b[0], ca, cb))


def silu(v):
    half = 0.5 * v
    return half + half * jnp.tanh(half)


def iota(shape, dim):
    return lax.broadcasted_iota(i32, shape, dim)


def turns(t):
    angle = two_pi * (t - jnp.floor(t + 0.5))
    return jnp.cos(angle), jnp.sin(angle)


def params(mebibytes=58):
    return pltpu.CompilerParams(vmem_limit_bytes=mebibytes << 20)


def cost(flops, transcendentals, moved):
    return pl.CostEstimate(flops=flops, transcendentals=transcendentals, bytes_accessed=moved)


SMEM = pl.BlockSpec(memory_space=pltpu.SMEM)


def up_kernel(feat, up, charge_weight, out, charges):
    charges[...] = dot(charge_weight[...], feat[:, 0:128], 1, 1)
    for b in range(2):
        for c in range(4):
            rows = feat[b * 128 : (b + 1) * 128, c * 128 : (c + 1) * 128]
            mapped = dot(up[min(c, 1)], rows, 0, 1).astype(bf16)
            for q in range(4):
                out[b, row_of(q, c) : row_of(q, c) + 32, :] = mapped[32 * q : 32 * (q + 1)]


def moment_kernel(
    dest, slot, charges_in, pos, species, halo, out, basis_high, basis_low, waves, basis, stage
):
    gx = lax.axis_index("gx").astype(f32)
    charges = charges_in[...]
    lane = iota((1, 256), 1)
    second = lane >= 128
    xyz = pos[...].astype(f32)
    along_x = xyz[0:1] + gx
    along_y = xyz[1:2] + jnp.where(second, dest[1], dest[0]).astype(f32)
    along_z = xyz[2:3]
    cos_x, sin_x = turns((iota((NX, 256), 0) + 1).astype(f32) * along_x * (1.0 / 8.0))
    cos_y, sin_y = turns((iota((NY, 256), 0) + 1).astype(f32) * along_y * (1.0 / 16.0))
    cos_z, sin_z = turns(iota((8, 256), 0).astype(f32) * along_z)
    pairs = [
        (cos_z[abs(z) : abs(z) + 1], sin_z[abs(z) : abs(z) + 1] * (1.0 if z >= 0 else -1.0))
        for z in range(-NZ, NZ + 1)
    ]
    for i, (c, s) in enumerate(pairs):
        at = i * 128
        basis[at : at + 32, 0:256] = cos_y * c
        basis[at + 32 : at + 64, 0:256] = sin_y * c
        basis[at + 64 : at + 96, 0:256] = cos_y * s
        basis[at + 96 : at + 128, 0:256] = sin_y * s
        basis[at : at + 32, 256:512] = -(cos_y * s)
        basis[at + 32 : at + 64, 256:512] = -(sin_y * s)
        basis[at + 64 : at + 96, 256:512] = cos_y * c
        basis[at + 96 : at + 128, 256:512] = sin_y * c
    at = 128 * (SLABS - 1)
    basis[at : at + 128, :] = jnp.zeros((128, 512), f32)
    for i, (c, s) in enumerate(pairs):
        basis[at + i : at + i + 1, 0:256] = c
        basis[at + i : at + i + 1, 256:512] = -s
        basis[at + 64 + i : at + 65 + i, 0:256] = s
        basis[at + 64 + i : at + 65 + i, 256:512] = c
    waves[0:8] = charges
    waves[8:24] = cos_x
    waves[24:40] = sin_x
    left_cos = (cos_x[:, None, :] * charges[None]).reshape(128, 256)
    left_sin = (sin_x[:, None, :] * charges[None]).reshape(128, 256)
    basis_high[...], basis_low[...] = halves(basis[...])
    left = halves(jnp.concatenate([left_cos, left_sin], axis=1))
    moments = dot_halves(left, (basis_high[...], basis_low[...]), 1, 1)
    for i in range(SLABS):
        stage[:, i, :] = moments[:, i * 128 : (i + 1) * 128]
    kinds = species[...].astype(f32)
    for b in range(2):
        cut = slice(b * 128, (b + 1) * 128)
        for m in range(3):
            stage[:, 6 + 3 * b + m, :] = jnp.broadcast_to(xyz[m : m + 1, cut], (128, 128))
        stage[:, 12 + b, :] = jnp.broadcast_to(kinds[:, cut], (128, 128))
    listed = jnp.concatenate([halo[...], jnp.zeros((1, 96), i32)], axis=1)
    at = iota((1, 128), 1)
    for b in range(2):
        listed = jnp.where(at == 32 + b, dest[b], listed)
        listed = jnp.where(at == 34 + b, slot[b], listed)
    stage[:, 14, :] = jnp.broadcast_to(listed.astype(f32), (128, 128))
    stage[:, 15, :] = jnp.zeros((128, 128), f32)
    out[...] = stage[...].astype(bf16)


def count_kernel(wave_index, out):
    own_x = (lax.axis_index("gx") * 16 + lax.axis_index("yz")) // 8 + 1
    kx, ky, kz = wave_index[0:1, :], wave_index[1:2, :], wave_index[2:3, :]
    count = kx.shape[1]
    ours = kx == own_x
    rank = iota((8, count), 0)
    z_rows = jnp.where(ours & (kz == rank - NZ), 1.0, 0.0).astype(bf16)
    flat_rows = jnp.where(ours & (ky == 0) & (rank == SLABS - 1), 1.0, 0.0).astype(bf16)
    z_any = jnp.where(kz == rank - NZ, 1.0, 0.0).astype(bf16)
    y_match = jnp.where(jnp.abs(ky) == iota((NY, count), 0) + 1, 1.0, 0.0)
    y_sign = jnp.where(ky < 0, -y_match, y_match)
    even = dot(z_rows, y_match.astype(bf16), 1, 1)
    odd = dot(z_rows, y_sign.astype(bf16), 1, 1)
    flat = dot(flat_rows, z_any, 1, 1)
    gap = jnp.zeros((8, 56), f32)
    even = jnp.concatenate([even] * 4, axis=1)
    odd = jnp.concatenate([odd] * 4, axis=1)
    flat = jnp.concatenate([flat, gap] * 2, axis=1)
    row, lane = iota((8, 128), 0), iota((8, 128), 1)
    in_flat = row == SLABS - 1
    x_wave = own_x.astype(f32) * (two_pi / 8.0)
    y_wave = jnp.where(in_flat, 0, lane % 32 + 1).astype(f32) * (two_pi / 16.0)
    z_wave = (jnp.where(in_flat, lane % 64, row) - NZ).astype(f32) * two_pi
    squared = x_wave * x_wave + y_wave * y_wave + z_wave * z_wave
    prefactor = 8.0 * math.pi * ewald_scale / 128.0
    weight = prefactor * jnp.exp(-0.5 * ewald_width * ewald_width * squared) / squared
    out[0:8] = weight * jnp.where(in_flat, flat, even)
    out[8:16] = weight * jnp.where(in_flat, 0.0, odd)


def weight_kernel(
    sent, weights, out, table_out, kinds_out, lists_out, home_out, stage
):
    stage[...] = sent[...].astype(f32)
    total = jnp.sum(stage[:, 0:8, :], axis=0)
    row, lane = iota((8, 128), 0), iota((8, 128), 1)
    total = jnp.where(row < SLABS, total, 0.0)
    far = pltpu.roll(total, 64, 1)
    group = lane // 32
    swapped = jnp.where(group % 2 == 0, pltpu.roll(far, 96, 1), pltpu.roll(far, 32, 1))
    swapped = jnp.where((group == 0) | (group == 3), -swapped, swapped)
    coefficient = total * weights[0:8] + swapped * weights[8:16]
    out[...] = jnp.broadcast_to(coefficient[None], out.shape)
    gx, yz = lax.axis_index("gx"), lax.axis_index("yz")
    targets = [
        (gx, yz),
        ((gx + 7) % 8, yz),
        ((gx + 1) % 8, yz),
        (gx, (yz + 15) % 16),
        (gx, (yz + 1) % 16),
    ]
    plan = jnp.transpose(stage[:, 14, :])
    row = iota((16, 128), 0)
    device = iota((16, 128), 1)
    want_x, want_y = jnp.full((16, 128), -1, i32), jnp.full((16, 128), -1, i32)
    for t, (tx, ty) in enumerate(targets):
        want_x = jnp.where(row // 2 == t, tx, want_x)
        want_y = jnp.where(row // 2 == t, ty, want_y)
    here = (device // 16 == want_x).astype(f32)
    want_y, want_slot = want_y.astype(f32), (row % 2).astype(f32)
    picks = []
    for b in range(2):
        match = (plan[32 + b : 33 + b] == want_y) & (plan[34 + b : 35 + b] == want_slot)
        picks.append(jnp.where(match, here, 0.0))
    exact = [pick.astype(bf16) for pick in picks]

    def from_home(first, step):
        return sum(
            dot(exact[b], stage[:, first + b * step, :].astype(bf16), 1, 0) for b in range(2)
        )

    xyz = [from_home(6 + m, 3) for m in range(3)]
    kinds = from_home(12, 1)
    kinds_out[...] = jnp.concatenate([kinds[0:1], kinds[1:2]], axis=1)
    both = picks[0] + picks[1]
    column = 2.0 * both * (device % 16).astype(f32) + picks[1]
    for i, r in enumerate((0, 1, 6, 7, 8, 9)):
        home_out[i] = jnp.sum(jnp.where(row == r, column, 0.0)).astype(i32)
    lane = iota((1, 128), 1)
    atom = iota((128, 128), 0)
    ghosts = jnp.zeros((8, 128), f32)
    for t, (tx, ty) in enumerate(targets[1:]):
        listed = stage[tx * 16 + ty, 14:15, :].astype(i32)
        if t:
            listed = pltpu.roll(listed, 32 * t, 1)
        listed = jnp.where(lane // 32 == t, listed, -1)
        lists_out[t : t + 1] = listed
        for s in range(2):
            at = 2 * (t + 1) + s
            rows = jnp.concatenate(
                [x[at : at + 1] for x in xyz] + [jnp.zeros((5, 128), f32)], axis=0
            )
            chosen = jnp.where(atom + 128 * s == listed, 1.0, 0.0).astype(bf16)
            ghosts = ghosts + dot(rows.astype(bf16), chosen, 1, 0)
    part = lane // 32
    shifts = [
        jnp.where(part == 0, -1.0, jnp.where(part == 1, 1.0, 0.0)),
        jnp.where(part == 2, -1.0, jnp.where(part == 3, 1.0, 0.0)),
        jnp.zeros((1, 128), f32),
    ]
    zero = jnp.zeros((1, 128), f32)
    rows = [v for m in range(3) for v in (xyz[m][0:1], xyz[m][1:2], ghosts[m : m + 1] + shifts[m])]
    table_out[...] = jnp.concatenate(rows + [zero] * 7, axis=0)


def field_kernel(
    coeffs,
    basis_high,
    basis_low,
    waves,
    feat,
    skip_weight,
    field_weight,
    read_weight,
    force_weight,
    out,
    stacked,
):
    lane = iota((128, 128), 1)
    group_even = (lane // 32) % 2 == 0
    low_half = lane < 64
    y_wave = (lane % 32 + 1).astype(f32) * (two_pi / 16.0)
    for i in range(SLABS):
        cut = slice(i * 128, (i + 1) * 128)
        c = coeffs[:, i, :]
        stacked[0:128, cut] = c
        half = pltpu.roll(c, 64, 1)
        if i < SLABS - 1:
            moved = jnp.where(group_even, pltpu.roll(c, 96, 1), -pltpu.roll(c, 32, 1))
            stacked[128:256, cut] = y_wave * moved
            z_wave = two_pi * (i - NZ)
        else:
            stacked[128:256, cut] = jnp.zeros((128, 128), f32)
            z_wave = (lane % 64 - NZ).astype(f32) * two_pi
        stacked[256:384, cut] = z_wave * jnp.where(low_half, half, -half)
    grid = dot_halves(halves(stacked[...]), (basis_high[...], basis_low[...]), 1, 0)
    charges = waves[0:8]
    cos_x = jnp.broadcast_to(waves[8:24][:, None, :], (NX, 8, 256)).reshape(128, 256)
    sin_x = jnp.broadcast_to(waves[24:40][:, None, :], (NX, 8, 256)).reshape(128, 256)
    x_wave = (iota((128, 256), 0) // 8 + 1).astype(f32) * (two_pi / 8.0)

    def channels(v):
        return jnp.sum(v.reshape(NX, 8, 256), axis=0)

    def even_part(at):
        return channels(cos_x * grid[at : at + 128, 0:256] + sin_x * grid[at : at + 128, 256:512])

    potential = even_part(0)
    field = [
        channels(x_wave * (sin_x * grid[0:128, 0:256] - cos_x * grid[0:128, 256:512])),
        -even_part(128),
        -even_part(256),
    ]
    scalars = dot(field_weight[...], potential, 0, 0, highest) + dot(
        skip_weight[0], feat[:, 0:128], 0, 1
    )
    out[0:16] = dot(read_weight[...].astype(f32), scalars, 1, 0, highest)
    for m in range(3):
        vector = dot(skip_weight[1], feat[:, (m + 1) * 128 : (m + 2) * 128], 0, 1)
        out[16 + m : 17 + m] = dot(force_weight[...], vector, 1, 0, highest) + jnp.sum(
            charges * field[m], axis=0, keepdims=True
        )
    out[19:20] = 0.5 * jnp.sum(charges * potential, axis=0, keepdims=True)
    out[20:24] = jnp.zeros((4, 256), f32)


def radial_kernel(
    table,
    neighbours,
    live,
    radial_in,
    radial_mid,
    hidden_out,
    offset_out,
    dist_stage,
    scale_stage,
):
    tables = [
        [jnp.broadcast_to(table[3 * m + i : 3 * m + i + 1], (8, 128)) for i in range(3)]
        for m in range(3)
    ]
    for n in range(0, 64, 8):
        for half in range(2):
            cut = slice(half * 128, (half + 1) * 128)
            index = neighbours[n : n + 8, cut]
            within, block = index & 127, index >> 7
            squared = jnp.zeros((8, 128), f32)
            for m in range(3):
                found = [
                    jnp.take_along_axis(table, within, axis=1, mode="promise_in_bounds")
                    for table in tables[m]
                ]
                picked = jnp.where(block == 0, found[0], jnp.where(block == 1, found[1], found[2]))
                offset = picked - tables[m][half]
                offset_out[m, n : n + 8, cut] = offset
                squared = squared + offset * offset
            dist = jnp.sqrt(squared)
            dist_stage[n : n + 8, cut] = dist
            u = dist * (1.0 / cutoff_radius)
            u6 = (u * u) * (u * u) * (u * u)
            envelope = 1.0 + u6 * (-28.0 + u * (48.0 - 21.0 * u))
            alive = iota((8, 128), 0) + n < live[:, cut]
            scale_stage[n : n + 8, cut] = jnp.where(alive, 0.125 * envelope, 0.0)
    first = jnp.transpose(radial_in[...].astype(f32)).astype(bf16)
    mid = [jnp.transpose(radial_mid[i].astype(f32)).astype(bf16) for i in range(2)]
    centre = iota((8, 256), 0).astype(f32) * (cutoff_radius / 7.0)

    def body(group, carry):
        start = group * RADIAL_GROUP
        rows = []
        for j in range(RADIAL_GROUP):
            away = dist_stage[pl.ds(start + j, 1), :] - centre
            rows.append(jnp.exp(-4.0 * (away * away)))
        hidden = silu(dot(first, jnp.concatenate(rows, axis=1).astype(bf16), 1, 0)).astype(bf16)
        hidden = silu(dot(mid[0], hidden, 1, 0)).astype(bf16)
        hidden = silu(dot(mid[1], hidden, 1, 0))
        for j in range(RADIAL_GROUP):
            scaled = hidden[:, j * 256 : (j + 1) * 256] * scale_stage[pl.ds(start + j, 1), :]
            hidden_out[start + j] = scaled.astype(bf16)
        return carry

    lax.fori_loop(0, 64 // RADIAL_GROUP, body, 0)


def spread_kernel(hidden, radial_out, out, spread):
    mapped = jnp.transpose(radial_out[...].astype(f32)).astype(bf16)
    for q in range(4):
        for c in range(4):
            at = 128 * c + 32 * q
            spread[row_of(q, c) : row_of(q, c) + 32] = mapped[at : at + 32]

    def body(group, carry):
        for j in range(SLOT_GROUP):
            n = group * SLOT_GROUP + j
            out[n] = dot(spread[...], hidden[n], 1, 0).astype(bf16)
        return carry

    lax.fori_loop(0, 64 // SLOT_GROUP, body, 0)


def near_kernel(home, own0, own1, low0, low1, high0, high1, lists, table):
    table[:, 0:128] = own0[0]
    table[:, 128:256] = own1[0]
    atom = iota((128, 128), 0)
    ghosts = jnp.zeros((512, 128), f32)
    for t, pair in ((2, (low0, low1)), (3, (high0, high1))):
        for s, block in enumerate(pair):
            chosen = jnp.where(atom + 128 * s == lists[t : t + 1], 1.0, 0.0).astype(bf16)
            ghosts = ghosts + dot(block[0], chosen, 1, 0)
    table[:, 256:384] = ghosts.astype(bf16)


def halo_kernel(home, first, second, halo, out):
    atom = iota((128, 32), 0)
    chosen = [jnp.where(atom + 128 * s == halo[...], 1.0, 0.0).astype(bf16) for s in range(2)]
    out[...] = (dot(chosen[0], first[0], 0, 1) + dot(chosen[1], second[0], 0, 1)).astype(bf16)


def message_kernel(
    home,
    near,
    left,
    right,
    neighbours,
    offsets,
    radials,
    kinds,
    prod_weight,
    out_weight,
    read_weight,
    force_weight,
    out,
    table,
    total,
):
    table[...] = near[...]
    even = lax.axis_index("gx") % 2 == 0
    pair = [jnp.transpose(ghost[...].astype(f32)) for ghost in (left, right)]
    table[:, 256:288] = jnp.where(even, pair[1], pair[0]).astype(bf16)
    table[:, 288:320] = jnp.where(even, pair[0], pair[1]).astype(bf16)
    total[...] = jnp.zeros((512, 256), f32)
    own_place = iota((256, 256), 0).astype(f32).astype(bf16)
    ghost_place = iota((128, 256), 0).astype(f32).astype(bf16)

    def choice(n):
        row = neighbours[pl.ds(n, 1), :]
        own = jnp.where(row < 256, row, -1).astype(f32).astype(bf16)
        ghost = (row - 256).astype(f32).astype(bf16)
        one, none = jnp.ones((), bf16), jnp.zeros((), bf16)
        return jnp.concatenate(
            [jnp.where(own_place == own, one, none), jnp.where(ghost_place == ghost, one, none)],
            axis=0,
        )

    def body(group, carry):
        slots = [group * SLOT_GROUP + j for j in range(SLOT_GROUP)]
        chosen = [choice(n) for n in slots]
        away = [[offsets[m, pl.ds(n, 1), :] for m in range(3)] for n in slots]
        for q in range(4):
            rows = slice(128 * q, 128 * (q + 1))
            cuts = [slice(row_of(q, c), row_of(q, c) + 32) for c in range(4)]
            sums = [total[cut] for cut in cuts]
            for j, r in enumerate(away):
                up = dot(table[rows], chosen[j], 1, 0)
                radial = radials[slots[j], rows].astype(f32)
                u = [up[32 * c : 32 * (c + 1)] for c in range(4)]
                path = [radial[32 * c : 32 * (c + 1)] for c in range(4)]
                along = u[1] * r[0] + u[2] * r[1] + u[3] * r[2]
                sums[0] = sums[0] + path[0] * u[0] + path[1] * along
                scalar = path[2] * u[0]
                for m in range(3):
                    sums[m + 1] = sums[m + 1] + scalar * r[m] + path[3] * u[m + 1]
            for cut, value in zip(cuts, sums):
                total[cut] = value
        return carry

    lax.fori_loop(0, 64 // SLOT_GROUP, body, 0)
    finish_messages(total, home, kinds, prod_weight, out_weight, read_weight, force_weight, out)


def finish_messages(
    total, home, kinds, prod_weight, out_weight, read_weight, force_weight, out
):
    kind = jnp.where(iota((6, 256), 0).astype(f32) == kinds[...], 1.0, 0.0)
    high, mid = halves(prod_weight[...])
    low = (prod_weight[...] - high.astype(f32) - mid.astype(f32)).astype(bf16)
    kind = kind.astype(bf16)
    paths = dot(high, kind, 0, 0) + (dot(mid, kind, 0, 0) + dot(low, kind, 0, 0))
    p = [paths[128 * i : 128 * (i + 1)] for i in range(5)]
    a0, *a1 = [
        jnp.concatenate([total[row_of(q, c) : row_of(q, c) + 32] for q in range(4)], axis=0)
        for c in range(4)
    ]
    square = a1[0] * a1[0] + a1[1] * a1[1] + a1[2] * a1[2]
    b0 = (p[0] * a0 + p[1] * a0 * a0 + p[2] * square).astype(bf16)
    rows = [dot(read_weight[...].astype(f32), dot(out_weight[0], b0, 0, 0), 1, 0, highest)]
    for m in range(3):
        b1 = (p[3] * a1[m] + p[4] * a0 * a1[m]).astype(bf16)
        rows.append(dot(force_weight[...], dot(out_weight[1], b1, 0, 0), 1, 0, highest))
    rows.append(jnp.zeros((5, 256), f32))
    result = jnp.concatenate(rows, axis=0)
    out[...] = jnp.zeros(out.shape, f32)
    for s in range(2):
        out[home[s] // 2] = result[:, s * 128 : (s + 1) * 128]


def final_kernel(dest, sent, own, read_vector, forces, energies):
    for b in range(2):
        cut = slice(b * 128, (b + 1) * 128)
        both = own[:, cut] + sent[dest[b]]
        forces[:, cut] = both[16:19]
        energies[:, cut] = (
            dot(read_vector[...], silu(both[0:16]), 1, 0, highest) + both[19:20]
        )


def whole(shape, dtype=f32):
    return jax.ShapeDtypeStruct(shape, dtype)


def blocks_of(shape):
    return pl.BlockSpec(shape, lambda i, home: (0,) * len(shape))


def on_device(
    positions,
    species,
    features,
    move_dest,
    move_slot,
    halo_list,
    neighbours,
    neighbour_count,
    wave_index,
    radial_in,
    radial_mid,
    radial_out,
    up_weight,
    prod_weight,
    out_weight,
    skip_weight,
    charge_weight,
    field_weight,
    read_weight,
    read_vector,
    force_weight,
):
    force_row = force_weight.reshape(1, 128)
    vmem = pl.BlockSpec(memory_space=pltpu.VMEM)

    read_rows = read_weight.T
    send_up, charges = pl.pallas_call(
        up_kernel,
        out_shape=(whole((2, 512, 128), bf16), whole((8, 256))),
        compiler_params=params(),
        cost_estimate=cost(1 << 25, 0, 1 << 20),
        name="up",
    )(features, up_weight, charge_weight.T)
    moved_up = lax.all_gather(send_up, "yz", axis=0, tiled=True)

    moments, basis_high, basis_low, waves = pl.pallas_call(
        moment_kernel,
        out_shape=(
            whole((128, 16, 128), bf16),
            whole((128 * SLABS, 512), bf16),
            whole((128 * SLABS, 512), bf16),
            whole((40, 256)),
        ),
        in_specs=[SMEM] * 2 + [vmem] * 4,
        scratch_shapes=[
            pltpu.VMEM((128 * SLABS, 512), f32),
            pltpu.VMEM((128, 16, 128), f32),
        ],
        compiler_params=params(20),
        cost_estimate=cost(1 << 30, 1 << 15, 3 << 20),
        name="moment",
    )(
        move_dest,
        move_slot,
        charges,
        positions,
        species.reshape(1, 256),
        halo_list.reshape(1, 32),
    )
    sent = lax.all_to_all(moments, ("gx", "yz"), 0, 0, tiled=True)
    weights = pl.pallas_call(
        count_kernel,
        out_shape=whole((16, 128)),
        compiler_params=params(12),
        cost_estimate=cost(1 << 28, 1 << 11, 1 << 18),
        name="count",
    )(wave_index)
    coeffs, table, kinds, lists, home = pl.pallas_call(
        weight_kernel,
        out_shape=(
            whole((128, 8, 128)),
            whole((16, 128)),
            whole((1, 256)),
            whole((4, 128), i32),
            whole((6,), i32),
        ),
        in_specs=[vmem, vmem],
        out_specs=(vmem, vmem, vmem, vmem, SMEM),
        scratch_shapes=[pltpu.VMEM((128, 16, 128), f32)],
        compiler_params=params(12),
        cost_estimate=cost(1 << 27, 1 << 11, 1 << 20),
        name="weight",
    )(sent, weights)
    coeffs = lax.all_to_all(coeffs, ("gx", "yz"), 0, 0, tiled=True)

    hidden, offsets = pl.pallas_call(
        radial_kernel,
        out_shape=(whole((64, 64, 256), bf16), whole((3, 64, 256))),
        scratch_shapes=[pltpu.VMEM((64, 256), f32), pltpu.VMEM((64, 256), f32)],
        compiler_params=params(20),
        cost_estimate=cost(1 << 32, 1 << 22, 4 << 20),
        name="radial",
    )(table, neighbours.T, neighbour_count.reshape(1, 256), radial_in, radial_mid)

    moved_up, hidden = lax.optimization_barrier((moved_up, hidden))
    nearby = [
        pl.BlockSpec((1, 512, 128), lambda i, home, at=at: (home[at], 0, 0)) for at in range(6)
    ]
    send_halo = pl.pallas_call(
        halo_kernel,
        out_shape=whole((32, 512), bf16),
        grid_spec=pltpu.PrefetchScalarGridSpec(
            num_scalar_prefetch=1,
            grid=(1,),
            in_specs=nearby[0:2] + [blocks_of((1, 32))],
            out_specs=blocks_of((32, 512)),
        ),
        compiler_params=params(61),
        cost_estimate=cost(1 << 24, 0, 1 << 18),
        name="halo",
    )(home, moved_up, moved_up, halo_list.reshape(1, 32))
    send_halo, late_hidden, late_up = lax.optimization_barrier((send_halo, hidden, moved_up))
    near = pl.pallas_call(
        near_kernel,
        out_shape=whole((512, 384), bf16),
        grid_spec=pltpu.PrefetchScalarGridSpec(
            num_scalar_prefetch=1,
            grid=(1,),
            in_specs=nearby + [blocks_of((4, 128))],
            out_specs=blocks_of((512, 384)),
        ),
        compiler_params=params(12),
        cost_estimate=cost(1 << 28, 0, 1 << 20),
        name="near",
    )(home, *[late_up] * 6, lists)
    radials = pl.pallas_call(
        spread_kernel,
        out_shape=whole((64, 512, 256), bf16),
        in_specs=[vmem, vmem],
        out_specs=vmem,
        scratch_shapes=[pltpu.VMEM((512, 64), bf16)],
        compiler_params=params(12),
        cost_estimate=cost(6 << 30, 0, 18 << 20),
        name="spread",
    )(late_hidden, radial_out)
    up = [(i, (i + 1) % 8) for i in range(8)]
    first = [pair for a, b in up[1::2] for pair in ((a, b), (b, a))]
    second = [pair for a, b in up[0::2] for pair in ((a, b), (b, a))]
    left = lax.ppermute(send_halo, "gx", second)
    right = lax.ppermute(send_halo, "gx", first)

    part = pl.pallas_call(
        field_kernel,
        out_shape=whole((24, 256)),
        scratch_shapes=[pltpu.VMEM((384, 128 * SLABS), f32)],
        compiler_params=params(20),
        cost_estimate=cost(1 << 31, 0, 3 << 20),
        name="field",
    )(coeffs, basis_high, basis_low, waves, features, skip_weight, field_weight, read_rows, force_row)

    returned = pl.pallas_call(
        message_kernel,
        out_shape=whole((16, 24, 128)),
        in_specs=[SMEM] + [vmem] * 11,
        out_specs=vmem,
        scratch_shapes=[pltpu.VMEM((512, 384), bf16), pltpu.VMEM((512, 256), f32)],
        compiler_params=params(12),
        cost_estimate=cost(12 << 30, 0, 4 << 20),
        name="message",
    )(
        home,
        near,
        left,
        right,
        neighbours.T,
        offsets,
        radials,
        kinds,
        prod_weight,
        out_weight,
        read_rows,
        force_row,
    )
    returned = lax.all_to_all(returned, "yz", 0, 0, tiled=True)
    forces, energies = pl.pallas_call(
        final_kernel,
        out_shape=(whole((3, 256)), whole((1, 256))),
        in_specs=[SMEM, vmem, vmem, vmem],
        compiler_params=params(12),
        cost_estimate=cost(1 << 14, 1 << 12, 1 << 16),
        name="final",
    )(move_dest, returned, part, read_vector.reshape(1, 16))
    return forces, energies.reshape(256)


def solution(mesh):
    whole_spec = P(("gx", "yz"))
    in_specs = (
        (P(None, ("gx", "yz")), whole_spec, P(("gx", "yz"), None))
        + (whole_spec,) * 3
        + (P(("gx", "yz"), None), whole_spec)
        + (P(),) * 13
    )
    out_specs = (P(None, ("gx", "yz")), whole_spec)
    return jax.shard_map(
        on_device, mesh=mesh, in_specs=in_specs, out_specs=out_specs, check_vma=False
    )
```
